512 devices in a mesh: member: 8 (over z_lo), node: 64 (over y, z_hi, x, core).
Axes of the slice: x: 4, y: 4, z: 16 (z_hi: 2, z_lo: 8; z = z_hi * 8 + z_lo), core: 2. Of those that a mesh axis runs over, the one named last changes fastest.
Arguments:
- vertex_embedding_array: bfloat16 [8, 262144, 128], P('member', 'node'), may hold values from -12 to 12
- result_sensitivity: bfloat16 [8, 262144, 128], P('member', 'node'), may hold values from -6 to 6
- hidden_projection: bfloat16 [128, 128], replicated, may hold values from -0.5 to 0.5
- aggregate_projection: bfloat16 [128, 128], replicated, may hold values from -0.5 to 0.5
- aggregate_offset: float32 [128], replicated, may hold values from -3 to 3
- assignment_projection: bfloat16 [16, 32], replicated, may hold values from -1.5 to 1.5
- softmax_sharpness: float32 [8], replicated, may hold values from 0.5 to 2
- state_asking_map: bfloat16 [16, 16], replicated, may hold values from -1.5 to 1.5
- state_lookup_map: bfloat16 [16, 16], replicated, may hold values from -1.5 to 1.5
- state_content_map: bfloat16 [16, 16], replicated, may hold values from -1.5 to 1.5
- result_projection: bfloat16 [128, 128], replicated, may hold values from -0.5 to 0.5
Outputs:
- vertex_sensitivity: float32 [8, 262144, 128], P('member', 'node')
- mid_grad: float32 [128, 128], replicated
- feature_grad: float32 [128, 128], replicated
- bias_grad: float32 [128], replicated
- slice_grad: float32 [16, 32], replicated
- temperature_grad: float32 [8], replicated
- query_grad: float32 [16, 16], replicated
- key_grad: float32 [16, 16], replicated
- value_grad: float32 [16, 16], replicated
- projection_grad: float32 [128, 128], replicated
The draws below stay inside these ranges and needn't reach their ends.
All inputs are finite; a program needn't handle non-finite values.
Results may differ from the reference program's by a relative error of at most 0.0054.
The reference program's roundings to bfloat16 on the way count: a program that leaves them out, or rounds other values in their place, can miss the bound.
Values sent between devices are 32-bit elements; how exact they have to be, the bound alone decides.
No kernel may reach another device: no remote copies, remote signals or barrier semaphores. Data moves between devices by JAX's collectives and lax.ppermute only.
A program may use at most 64 MiB of HBM per device.

```python
import math
import jax
import jax.numpy as jnp
from jax import lax

MODEL_WIDTH = 128
NUM_CHANNELS = 8
M = 32
D = 16
NODES = 262144
MEMBERS = 8


def draw_vertex_embedding_array(key, part):
    subkeys = jax.random.split(key, 3)
    centres = jax.random.normal(subkeys[0], (MEMBERS, 16, MODEL_WIDTH), jnp.float32)
    labels = jax.random.randint(subkeys[1], (MEMBERS, NODES), 0, 16)
    picked = jax.vmap(lambda centre_table, label_rows: centre_table[label_rows])(centres, labels)
    jitter = jax.random.normal(subkeys[2], (MEMBERS, NODES, MODEL_WIDTH), jnp.float32)
    return jnp.clip(1.5 * picked + jitter, -12.0, 12.0).astype(jnp.bfloat16)


def shard_levels(key, dims, cuts, low, top_value):
    factor_of = 1.0
    for position, parts in cuts:
        heights = jax.random.uniform(jax.random.fold_in(jax.random.fold_in(key, 6), position), (parts,), jnp.float32, low / len(cuts), top_value / len(cuts))
        factor_of = factor_of * jnp.repeat(jnp.exp(heights), dims[position] // parts).reshape((-1,) + (1,) * (len(dims) - 1 - position))
    return factor_of


def bell_draw(own_key, dims, width, reach, shards=(), dtype=jnp.bfloat16):
    drawn = jax.random.normal(own_key, dims, jnp.float32) * width
    if len(shards) > 0:
        drawn = shard_levels(own_key, dims, shards, -0.22, 0.18) * drawn
    return jnp.clip(drawn, min=-reach, max=reach).astype(dtype)


def setup_inputs(seed: int = 0) -> dict:
    seeds = jax.random.split(jax.random.key(seed), 12)
    vertex_embedding_array = draw_vertex_embedding_array(jax.random.fold_in(seeds[11], 71), 0)
    result_sensitivity = bell_draw(seeds[1], (MEMBERS, NODES, MODEL_WIDTH), 1.0, 6.0, ((0, 8), (1, 64)))
    hidden_projection = bell_draw(seeds[2], (MODEL_WIDTH, MODEL_WIDTH), MODEL_WIDTH ** -0.5, 0.5)
    aggregate_projection = bell_draw(seeds[3], (MODEL_WIDTH, MODEL_WIDTH), MODEL_WIDTH ** -0.5, 0.5)
    aggregate_offset = bell_draw(seeds[4], (MODEL_WIDTH,), 0.5, 3.0, (), jnp.float32)
    assignment_projection = bell_draw(seeds[5], (D, M), D ** -0.5, 1.5)
    softmax_sharpness = jnp.clip(jnp.exp(jax.random.uniform(seeds[6], (NUM_CHANNELS,), jnp.float32, math.log(0.5), math.log(2.0))), 0.5, 2.0)
    state_asking_map = bell_draw(seeds[7], (D, D), D ** -0.5, 1.5)
    state_lookup_map = bell_draw(seeds[8], (D, D), D ** -0.5, 1.5)
    state_content_map = bell_draw(seeds[9], (D, D), D ** -0.5, 1.5)
    result_projection = bell_draw(seeds[10], (MODEL_WIDTH, MODEL_WIDTH), MODEL_WIDTH ** -0.5, 0.5)
    return {"vertex_embedding_array": vertex_embedding_array, "result_sensitivity": result_sensitivity, "hidden_projection": hidden_projection, "aggregate_projection": aggregate_projection, "aggregate_offset": aggregate_offset, "assignment_projection": assignment_projection, "softmax_sharpness": softmax_sharpness, "state_asking_map": state_asking_map, "state_lookup_map": state_lookup_map, "state_content_map": state_content_map, "result_projection": result_projection}


epsilon = 1e-05

def attend(physical_state_vectors, state_asking_map, state_lookup_map, state_content_map):
    exact_arithmetic_mode = lax.Precision.HIGHEST
    asking_vectors = jnp.einsum('uzi,ib->uzb', physical_state_vectors, state_asking_map, precision=exact_arithmetic_mode)
    random_seed_list = jnp.einsum('uzi,ib->uzb', physical_state_vectors, state_lookup_map, precision=exact_arithmetic_mode)
    content_vectors = jnp.einsum('uzi,ib->uzb', physical_state_vectors, state_content_map, precision=exact_arithmetic_mode)
    assignment_shares = jnp.einsum('hme,hke->hmk', asking_vectors, random_seed_list, precision=exact_arithmetic_mode) / math.sqrt(physical_state_vectors.shape[-1])
    expon = jnp.exp(assignment_shares)
    attention_rows = expon / lax.optimization_barrier(jnp.sum(expon, -1, keepdims=True))
    return jnp.einsum('lso,log->lsg', attention_rows, content_vectors, precision=exact_arithmetic_mode)

def single_ensemble_evaluation(channel_embedding, incoming_sensitivity, hidden_projection, aggregate_projection, aggregate_offset, assignment_projection, softmax_sharpness, state_asking_map, state_lookup_map, state_content_map, result_projection):
    exact_arithmetic_mode = lax.Precision.HIGHEST
    mesh_node_rows = channel_embedding.shape[0]
    mid_half = jnp.dot(channel_embedding, hidden_projection, preferred_element_type=jnp.float32).astype(jnp.bfloat16).reshape(mesh_node_rows, NUM_CHANNELS, D)
    feature_halfway = (jnp.dot(channel_embedding, aggregate_projection, preferred_element_type=jnp.float32) + aggregate_offset).astype(jnp.bfloat16).reshape(mesh_node_rows, NUM_CHANNELS, D)
    assignment_shares = jnp.einsum('nhd,dm->nhm', mid_half.astype(jnp.float32), assignment_projection.astype(jnp.float32), precision=exact_arithmetic_mode)
    assignment_energies = assignment_shares / softmax_sharpness[None, :, None]
    expon = jnp.exp(assignment_energies)
    probs = expon / lax.optimization_barrier(jnp.sum(expon, -1, keepdims=True))
    probability_halfway = probs.astype(jnp.bfloat16)
    pooled_numerator = jnp.einsum('wou,wog->oug', probability_halfway.astype(jnp.float32), feature_halfway.astype(jnp.float32), precision=exact_arithmetic_mode)
    denominator = lax.optimization_barrier(jnp.sum(probs, 0))
    physical_state_vectors = pooled_numerator / (denominator[:, :, None] + epsilon)
    token_out, attend_back = jax.vjp(attend, physical_state_vectors, state_asking_map.astype(jnp.float32), state_lookup_map.astype(jnp.float32), state_content_map.astype(jnp.float32))
    tokens_halfway = token_out.astype(jnp.bfloat16)
    mixed_tokens = jnp.einsum('afq,fqx->afx', probability_halfway.astype(jnp.float32), tokens_halfway.astype(jnp.float32), precision=exact_arithmetic_mode)
    mixed_half = mixed_tokens.reshape(mesh_node_rows, MODEL_WIDTH).astype(jnp.bfloat16)
    backward_halfway = jnp.dot(incoming_sensitivity, result_projection.T, preferred_element_type=jnp.float32).astype(jnp.bfloat16).reshape(mesh_node_rows, NUM_CHANNELS, D)
    mapping_contribution = jnp.dot(mixed_half.T, incoming_sensitivity, preferred_element_type=jnp.float32)
    slice_token_gradient = jnp.einsum('wou,wog->oug', probability_halfway.astype(jnp.float32), backward_halfway.astype(jnp.float32), precision=exact_arithmetic_mode)
    piece_reverse_derivative, asking_contribution, lookup_contribution, content_contribution = attend_back(slice_token_gradient)
    inverse = 1.0 / (denominator + epsilon)
    numerator_halfway = (piece_reverse_derivative * inverse[:, :, None]).astype(jnp.bfloat16)
    denom_back = -lax.optimization_barrier(jnp.sum(piece_reverse_derivative * physical_state_vectors, -1)) * inverse
    probability_backward = jnp.einsum('yrq,req->yre', backward_halfway.astype(jnp.float32), tokens_halfway.astype(jnp.float32), precision=exact_arithmetic_mode)
    probability_backward = probability_backward + jnp.einsum('yrq,req->yre', feature_halfway.astype(jnp.float32), numerator_halfway.astype(jnp.float32), precision=exact_arithmetic_mode)
    probability_backward = probability_backward + denom_back[None]
    feature_backward = jnp.einsum('afq,fqx->afx', probability_halfway.astype(jnp.float32), numerator_halfway.astype(jnp.float32), precision=exact_arithmetic_mode).reshape(mesh_node_rows, MODEL_WIDTH)
    shift_term_derivative = lax.optimization_barrier(jnp.sum(feature_backward, 0))
    feat_back_half = feature_backward.astype(jnp.bfloat16)
    inner = lax.optimization_barrier(jnp.sum(probs * probability_backward, -1, keepdims=True))
    assignment_energy_adjoint = probs * (probability_backward - inner)
    inverse_spread_derivative = -lax.optimization_barrier(jnp.sum(assignment_energy_adjoint * assignment_energies, axis=(0, 2))) / softmax_sharpness
    assignment_partial_result = (assignment_energy_adjoint / softmax_sharpness[None, :, None]).astype(jnp.bfloat16)
    division_term_derivative = jnp.einsum('nhd,nhm->dm', mid_half.astype(jnp.float32), assignment_partial_result.astype(jnp.float32), precision=exact_arithmetic_mode)
    mid_back_half = jnp.einsum('nhm,dm->nhd', assignment_partial_result.astype(jnp.float32), assignment_projection.astype(jnp.float32), precision=exact_arithmetic_mode).reshape(mesh_node_rows, MODEL_WIDTH).astype(jnp.bfloat16)
    hidden_contribution = jnp.dot(channel_embedding.T, mid_back_half, preferred_element_type=jnp.float32)
    channel_contribution = jnp.dot(channel_embedding.T, feat_back_half, preferred_element_type=jnp.float32)
    vertex_sensitivity = jnp.dot(mid_back_half, hidden_projection.T, preferred_element_type=jnp.float32) + jnp.dot(feat_back_half, aggregate_projection.T, preferred_element_type=jnp.float32)
    return (vertex_sensitivity, hidden_contribution, channel_contribution, shift_term_derivative, division_term_derivative, inverse_spread_derivative, asking_contribution, lookup_contribution, content_contribution, mapping_contribution)

def reference(vertex_embedding_array, result_sensitivity, hidden_projection, aggregate_projection, aggregate_offset, assignment_projection, softmax_sharpness, state_asking_map, state_lookup_map, state_content_map, result_projection):

    def one_member(layer_arguments):
        return single_ensemble_evaluation(layer_arguments[0], layer_arguments[1], hidden_projection, aggregate_projection, aggregate_offset, assignment_projection, softmax_sharpness, state_asking_map, state_lookup_map, state_content_map, result_projection)
    results = lax.map(one_member, (vertex_embedding_array, result_sensitivity))
    return (results[0], lax.optimization_barrier(jnp.sum(results[1], 0)), lax.optimization_barrier(jnp.sum(results[2], 0)), lax.optimization_barrier(jnp.sum(results[3], 0)), lax.optimization_barrier(jnp.sum(results[4], 0)), lax.optimization_barrier(jnp.sum(results[5], 0)), lax.optimization_barrier(jnp.sum(results[6], 0)), lax.optimization_barrier(jnp.sum(results[7], 0)), lax.optimization_barrier(jnp.sum(results[8], 0)), lax.optimization_barrier(jnp.sum(results[9], 0)))
```

```python
import math

import jax
import jax.numpy as jnp
from jax import lax
from jax.sharding import Mesh, PartitionSpec as P

MODEL_WIDTH = 128
NUM_CHANNELS = 8
D = 16


epsilon = 1e-05

NODE = ("y", "zh", "x", "core")
PLANE = ("y", "x", "core")
COLUMN = ("zl", "zh")
TOKEN_ROWS = 66
GRAD_ROWS = 416


def exchange(block, axes, copies):
    sent = jnp.broadcast_to(block[None], (copies,) + block.shape)
    return lax.all_to_all(sent, axes, 0, 0, tiled=True)


def sum_over_nodes(rows):
    half = TOKEN_ROWS // 2
    halves = rows.reshape(1, 2, half, 128)
    sent = jnp.broadcast_to(halves, (2, 2, half, 128)).reshape(4, half, 128)
    part = jnp.sum(lax.all_to_all(sent, ("zh", "core"), 0, 0, tiled=True), 0)
    part = jnp.sum(exchange(part, ("y", "x"), 16), 0)
    return lax.all_gather(part, "core", axis=0, tiled=True)


def sum_over_all(rows):
    parts = lax.all_to_all(rows.reshape(32, GRAD_ROWS // 32, 128), PLANE, 0, 0, tiled=True)
    part = jnp.sum(parts, 0)
    part = jnp.sum(exchange(part, COLUMN, 16), 0)
    return exchange(part, PLANE, 32).reshape(GRAD_ROWS, 128)


def pack(arrays, rows):
    flat = jnp.concatenate([a.reshape(-1) for a in arrays])
    return jnp.pad(flat, (0, rows * 128 - flat.shape[0])).reshape(rows, 128)


def unpack(rows, shapes):
    flat = rows.reshape(-1)
    out = []
    at = 0
    for shape in shapes:
        size = math.prod(shape)
        out.append(flat[at : at + size].reshape(shape))
        at += size
    return out


def attend(physical_state_vectors, state_asking_map, state_lookup_map, state_content_map):
    exact_arithmetic_mode = lax.Precision.HIGHEST
    asking_vectors = jnp.einsum(
        "uzi,ib->uzb", physical_state_vectors, state_asking_map, precision=exact_arithmetic_mode
    )
    random_seed_list = jnp.einsum(
        "uzi,ib->uzb", physical_state_vectors, state_lookup_map, precision=exact_arithmetic_mode
    )
    content_vectors = jnp.einsum(
        "uzi,ib->uzb", physical_state_vectors, state_content_map, precision=exact_arithmetic_mode
    )
    assignment_shares = jnp.einsum(
        "hme,hke->hmk", asking_vectors, random_seed_list, precision=exact_arithmetic_mode
    ) / math.sqrt(physical_state_vectors.shape[-1])
    expon = jnp.exp(assignment_shares)
    attention_rows = expon / jnp.sum(expon, -1, keepdims=True)
    return jnp.einsum(
        "lso,log->lsg", attention_rows, content_vectors, precision=exact_arithmetic_mode
    )


def shards(
    vertex_embedding_array,
    result_sensitivity,
    hidden_projection,
    aggregate_projection,
    aggregate_offset,
    assignment_projection,
    softmax_sharpness,
    state_asking_map,
    state_lookup_map,
    state_content_map,
    result_projection,
):
    channel_embedding = vertex_embedding_array[0]
    incoming_sensitivity = result_sensitivity[0]
    mesh_node_rows = channel_embedding.shape[0]
    mid_half = (
        jnp.dot(channel_embedding, hidden_projection, preferred_element_type=jnp.float32)
        .astype(jnp.bfloat16)
        .reshape(mesh_node_rows, NUM_CHANNELS, D)
    )
    feature_halfway = (
        (
            jnp.dot(channel_embedding, aggregate_projection, preferred_element_type=jnp.float32)
            + aggregate_offset
        )
        .astype(jnp.bfloat16)
        .reshape(mesh_node_rows, NUM_CHANNELS, D)
    )
    assignment_shares = jnp.einsum(
        "nhd,dm->nhm", mid_half, assignment_projection, preferred_element_type=jnp.float32
    )
    assignment_energies = assignment_shares / softmax_sharpness[None, :, None]
    expon = jnp.exp(assignment_energies)
    probs = expon / jnp.sum(expon, -1, keepdims=True)
    probability_halfway = probs.astype(jnp.bfloat16)
    pooled_numerator = jnp.einsum(
        "wou,wog->oug", probability_halfway, feature_halfway, preferred_element_type=jnp.float32
    )
    denominator = jnp.sum(probs, 0)
    backward_halfway = (
        jnp.dot(incoming_sensitivity, result_projection.T, preferred_element_type=jnp.float32)
        .astype(jnp.bfloat16)
        .reshape(mesh_node_rows, NUM_CHANNELS, D)
    )
    slice_token_gradient = jnp.einsum(
        "wou,wog->oug", probability_halfway, backward_halfway, preferred_element_type=jnp.float32
    )
    pooled = (pooled_numerator, slice_token_gradient, denominator)
    pooled_numerator, slice_token_gradient, denominator = unpack(
        sum_over_nodes(pack(pooled, TOKEN_ROWS)), [a.shape for a in pooled]
    )
    physical_state_vectors = pooled_numerator / (denominator[:, :, None] + epsilon)
    token_out, attend_back = jax.vjp(
        attend,
        physical_state_vectors,
        state_asking_map.astype(jnp.float32),
        state_lookup_map.astype(jnp.float32),
        state_content_map.astype(jnp.float32),
    )
    tokens_halfway = token_out.astype(jnp.bfloat16)
    mixed_half = (
        jnp.einsum(
            "afq,fqx->afx", probability_halfway, tokens_halfway, preferred_element_type=jnp.float32
        )
        .reshape(mesh_node_rows, MODEL_WIDTH)
        .astype(jnp.bfloat16)
    )
    mapping_contribution = jnp.dot(
        mixed_half.T, incoming_sensitivity, preferred_element_type=jnp.float32
    )
    piece_reverse_derivative, asking_contribution, lookup_contribution, content_contribution = (
        attend_back(slice_token_gradient)
    )
    inverse = 1.0 / (denominator + epsilon)
    numerator_halfway = (piece_reverse_derivative * inverse[:, :, None]).astype(jnp.bfloat16)
    denom_back = -jnp.sum(piece_reverse_derivative * physical_state_vectors, -1) * inverse
    probability_backward = jnp.einsum(
        "yrq,req->yre", backward_halfway, tokens_halfway, preferred_element_type=jnp.float32
    )
    probability_backward = probability_backward + jnp.einsum(
        "yrq,req->yre", feature_halfway, numerator_halfway, preferred_element_type=jnp.float32
    )
    probability_backward = probability_backward + denom_back[None]
    feature_backward = jnp.einsum(
        "afq,fqx->afx", probability_halfway, numerator_halfway, preferred_element_type=jnp.float32
    ).reshape(mesh_node_rows, MODEL_WIDTH)
    shift_term_derivative = jnp.sum(feature_backward, 0)
    feat_back_half = feature_backward.astype(jnp.bfloat16)
    inner = jnp.sum(probs * probability_backward, -1, keepdims=True)
    assignment_energy_adjoint = probs * (probability_backward - inner)
    inverse_spread_derivative = (
        -jnp.sum(assignment_energy_adjoint * assignment_energies, axis=(0, 2)) / softmax_sharpness
    )
    assignment_partial_result = (
        assignment_energy_adjoint / softmax_sharpness[None, :, None]
    ).astype(jnp.bfloat16)
    division_term_derivative = jnp.einsum(
        "nhd,nhm->dm", mid_half, assignment_partial_result, preferred_element_type=jnp.float32
    )
    mid_back_half = (
        jnp.einsum(
            "nhm,dm->nhd",
            assignment_partial_result,
            assignment_projection,
            preferred_element_type=jnp.float32,
        )
        .reshape(mesh_node_rows, MODEL_WIDTH)
        .astype(jnp.bfloat16)
    )
    hidden_contribution = jnp.dot(
        channel_embedding.T, mid_back_half, preferred_element_type=jnp.float32
    )
    channel_contribution = jnp.dot(
        channel_embedding.T, feat_back_half, preferred_element_type=jnp.float32
    )
    vertex_sensitivity = jnp.dot(
        mid_back_half, hidden_projection.T, preferred_element_type=jnp.float32
    ) + jnp.dot(feat_back_half, aggregate_projection.T, preferred_element_type=jnp.float32)
    dominant_summands = (hidden_contribution, channel_contribution, mapping_contribution)
    trailing_summands = (shift_term_derivative, division_term_derivative, inverse_spread_derivative)
    token_terms = tuple(
        term * (1.0 / 64.0)
        for term in (asking_contribution, lookup_contribution, content_contribution)
    )
    terms = dominant_summands + trailing_summands + token_terms
    totalled = unpack(sum_over_all(pack(terms, GRAD_ROWS)), [a.shape for a in terms])
    large_sums = totalled[:3]
    small_sums = totalled[3:6]
    piece_totals = totalled[6:]
    return (
        vertex_sensitivity[None],
        large_sums[0],
        large_sums[1],
        small_sums[0],
        small_sums[1],
        small_sums[2],
        piece_totals[0],
        piece_totals[1],
        piece_totals[2],
        large_sums[2],
    )


def solution(mesh):
    fine = Mesh(mesh.devices.reshape(8, 4, 2, 4, 2), ("zl",) + NODE)
    placed = (
        P("zl", NODE, None),
        P("zl", NODE, None),
        P(),
        P(),
        P(),
        P(),
        P(),
        P(),
        P(),
        P(),
        P(),
    )
    return jax.shard_map(
        shards,
        mesh=fine,
        in_specs=placed,
        out_specs=(P("zl", NODE, None), P(), P(), P(), P(), P(), P(), P(), P(), P()),
        check_vma=False,
    )
```

```python
import jax
import jax.numpy as jnp
from jax import lax
from jax.experimental import pallas as pl
from jax.experimental.pallas import tpu as pltpu
from jax.sharding import Mesh, PartitionSpec as P

HEADS = 8
SLICES = 32
D = 16
WIDTH = HEADS * D
LANES = HEADS * SLICES
EPS = 1e-05
TILE = 1024
NODE = ("y", "zh", "x", "core")
PLANE = ("y", "x", "core")
COLUMN = ("zl", "zh")
F32 = jnp.float32
BF16 = jnp.bfloat16
EXACT = lax.Precision.HIGHEST


def dot(a, b, ca=1, cb=0, precision=None):
    return lax.dot_general(
        a, b, (((ca,), (cb,)), ((), ())), precision=precision, preferred_element_type=F32
    )


def grid_of(shape):
    return lax.broadcasted_iota(jnp.int32, shape, 0), lax.broadcasted_iota(jnp.int32, shape, 1)


def match(shape, f, g):
    r, c = grid_of(shape)
    return f(r) == g(c)


def head16(i):
    return i >> 4


def head32(i):
    return i >> 5


def in16(i):
    return i & 15


def in32(i):
    return i & 31


def same(i):
    return i


def block_slices(a16x32):
    rows = dot(match((WIDTH, D), in16, same).astype(BF16), a16x32).astype(BF16)
    wide = dot(rows, match((SLICES, LANES), same, in32).astype(BF16))
    return jnp.where(match((WIDTH, LANES), head16, head32), wide, 0.0)


def block_square(a16x16):
    rows = dot(match((WIDTH, D), in16, same).astype(BF16), a16x16).astype(BF16)
    wide = dot(rows, match((D, WIDTH), same, in16).astype(BF16))
    return jnp.where(match((WIDTH, WIDTH), head16, head16), wide, 0.0)


def sharpness_row(sharp):
    col = lax.broadcasted_iota(jnp.int32, (1, LANES), 1) >> 5
    row = jnp.zeros((1, LANES), F32)
    for h in range(HEADS):
        row = jnp.where(col == h, sharp[h], row)
    return 1.0 / row


def group_sum(a, ones):
    high = a.astype(BF16)
    low = (a - high.astype(F32)).astype(BF16)
    return dot(high, ones) + dot(low, ones)


def fold_rows(a, rows):
    return jnp.sum(a.reshape(a.shape[0] // rows, rows, a.shape[1]), 0)


def stack_heads(a):
    tall = jnp.concatenate([a] * HEADS, 0)
    return jnp.where(match((LANES, WIDTH), head32, head16), tall, 0.0)


def pool_kernel(
    sharp, x, g, hidden, aggregate, offset, assign, result, probs_out, rows_out, pool_out,
    weights, assign_wide, scale, ones, pooled, mass,
):
    step = pl.program_id(0)

    @pl.when(step == 0)
    def _():
        weights[:, :WIDTH] = hidden[...]
        weights[:, WIDTH:] = aggregate[...]
        assign_wide[...] = block_slices(assign[...]).astype(BF16)
        scale[...] = sharpness_row(sharp)
        ones[...] = match((LANES, LANES), head32, head32).astype(BF16)
        pooled[...] = jnp.zeros_like(pooled)
        mass[...] = jnp.zeros_like(mass)

    both = dot(x[...], weights[...])
    mid = both[:, :WIDTH].astype(BF16)
    feat = (both[:, WIDTH:] + offset[...]).astype(BF16)
    back = dot(g[...], result[...], 1, 1).astype(BF16)
    rows_out[:, :WIDTH] = mid
    rows_out[:, WIDTH : 2 * WIDTH] = back
    rows_out[:, 2 * WIDTH :] = feat
    expon = jnp.exp(dot(mid, assign_wide[...]) * scale[...])
    probs = expon / group_sum(expon, ones[...])
    probs_out[...] = probs
    mass[...] += fold_rows(probs, 8)
    pooled[...] += dot(probs.astype(BF16), jnp.concatenate([back, feat], 1), 0, 0)

    @pl.when(step == pl.num_programs(0) - 1)
    def _():
        row, col = grid_of((LANES, LANES))
        kept = jnp.where((row >> 5) == ((col & 127) >> 4), pooled[...], 0.0)
        small = fold_rows(kept, SLICES)
        total = jnp.sum(mass[...], 0, keepdims=True)
        for z in range(2):
            pool_out[2 * z, :SLICES] = small[:, WIDTH:]
            pool_out[2 * z, SLICES:] = total[:, :WIDTH]
            pool_out[2 * z + 1, :SLICES] = small[:, :WIDTH]
            pool_out[2 * z + 1, SLICES:] = total[:, WIDTH:]


def attend_terms(pool, ask, look, content):
    numer = pool[0, :SLICES]
    token_grad = pool[1, :SLICES]
    mass = jnp.concatenate([pool[0, SLICES:], pool[1, SLICES:]], 1)
    spread = jnp.where(match((SLICES, LANES), same, in32), mass, 0.0)
    heads = match((LANES, WIDTH), head32, head16).astype(F32)
    lanes = match((LANES, LANES), head32, head32).astype(F32)
    denom = dot(spread, heads, precision=EXACT) + EPS
    inverse = 1.0 / denom
    tokens = numer / denom
    maps = [block_square(m[...]) for m in (ask, look, content)]
    q, k, v = [dot(tokens, m, precision=EXACT) for m in maps]
    keys = stack_heads(k)
    values = stack_heads(v)
    expon = jnp.exp(dot(q, keys, 1, 1, precision=EXACT) * 0.25)
    rows = expon / dot(expon, lanes, precision=EXACT)
    token_out = dot(rows, values, precision=EXACT)
    rows_back = dot(token_grad, values, 1, 1, precision=EXACT)
    centre = dot(rows_back * rows, lanes, precision=EXACT)
    scores_back = rows * (rows_back - centre) * 0.25
    q_back = dot(scores_back, keys, precision=EXACT)
    keep = match((LANES, WIDTH), head32, head16)
    k_back = fold_rows(jnp.where(keep, dot(scores_back, q, 0, 0, precision=EXACT), 0.0), SLICES)
    v_back = fold_rows(jnp.where(keep, dot(rows, token_grad, 0, 0, precision=EXACT), 0.0), SLICES)
    tok_back = sum(
        dot(b, m, 1, 1, precision=EXACT) for b, m in zip((q_back, k_back, v_back), maps)
    )
    numer_back = tok_back * inverse
    folded = dot(tok_back * tokens * inverse, heads, 1, 1, precision=EXACT)
    folded = jnp.where(match((SLICES, LANES), same, in32), folded, 0.0)
    denom_back = -jnp.sum(folded, 0, keepdims=True)
    square = match((WIDTH, WIDTH), head16, head16)
    lanes16 = match((WIDTH, WIDTH), in16, same).astype(F32)
    grads = []
    for b in (q_back, k_back, v_back):
        wide = jnp.where(square, dot(tokens, b, 0, 0, precision=EXACT), 0.0)
        grads.append(dot(fold_rows(wide, D), lanes16, precision=EXACT))
    return token_out, numer_back, denom_back, grads


def back_kernel(
    sharp, pool, hidden, aggregate, assign, ask, look, content, x, g, probs_in, rows_in,
    sense_out, grads_out,
    weights, assign_wide, scale, ones, token_wide, denom_back, small,
    sum_pair, sum_result, sum_slice, sum_bias, sum_heat,
):
    step = pl.program_id(0)

    @pl.when(step == 0)
    def _():
        weights[:, :WIDTH] = hidden[...]
        weights[:, WIDTH:] = aggregate[...]
        assign_wide[...] = block_slices(assign[...]).astype(BF16)
        scale[...] = sharpness_row(sharp)
        ones[...] = match((LANES, LANES), head32, head32).astype(BF16)
        token_out, numer_back, shift, grads = attend_terms(pool, ask, look, content)
        token_wide[:, :WIDTH] = stack_heads(token_out).astype(BF16)
        token_wide[:, WIDTH:] = stack_heads(numer_back).astype(BF16)
        denom_back[...] = shift
        small[...] = jnp.zeros_like(small)
        lane = lax.broadcasted_iota(jnp.int32, (D, WIDTH), 1)
        for i, term in enumerate(grads):
            moved = term if i == 0 else pltpu.roll(term, i * D, 1)
            part = jnp.where((lane >> 4) == i, moved, 0.0)
            small[:D, :] += part * (1.0 / 64.0)
        for ref in (sum_pair, sum_result, sum_slice, sum_bias, sum_heat):
            ref[...] = jnp.zeros_like(ref)

    mid = rows_in[:, :WIDTH]
    probs = probs_in[...]
    prob_back = dot(rows_in[:, WIDTH:], token_wide[...], 1, 1) + denom_back[...]
    inner = group_sum(probs * prob_back, ones[...])
    logit_back = probs * (prob_back - inner)
    sum_heat[...] += fold_rows(logit_back * dot(mid, assign_wide[...]), 8)
    score_back = (logit_back * scale[...]).astype(BF16)
    sum_slice[...] += dot(mid, score_back, 0, 0)
    mid_back = dot(score_back, assign_wide[...], 1, 1).astype(BF16)
    spread = dot(probs.astype(BF16), token_wide[...])
    mixed = spread[:, :WIDTH].astype(BF16)
    feat_wide = spread[:, WIDTH:]
    sum_bias[...] += fold_rows(feat_wide, 8)
    pair = jnp.concatenate([mid_back, feat_wide.astype(BF16)], 1)
    sum_result[...] += dot(mixed, g[...], 0, 0)
    sum_pair[...] += dot(x[...], pair, 0, 0)
    sense_out[...] = dot(pair, weights[...], 1, 1)

    @pl.when(step == pl.num_programs(0) - 1)
    def _():
        kept = jnp.where(match((WIDTH, LANES), head16, head32), sum_slice[...], 0.0)
        onto = (in32(grid_of((LANES, WIDTH))[0]) + 64) == grid_of((LANES, WIDTH))[1]
        small[:D, :] += dot(fold_rows(kept, D), onto.astype(F32), precision=EXACT)
        small[D : D + 1, :] = jnp.sum(sum_bias[...], 0, keepdims=True)
        heat = jnp.sum(sum_heat[...], 0, keepdims=True) * scale[...] * scale[...]
        heads = match((LANES, WIDTH), head32, same).astype(F32)
        heat = dot(jnp.broadcast_to(heat, (8, LANES)), heads, precision=EXACT)
        small[D + 1 : D + 2, :] = -heat[:1]
        for k in range(32):
            grads_out[k, 0:4, :] = sum_pair[4 * k : 4 * k + 4, :WIDTH]
            grads_out[k, 4:8, :] = sum_pair[4 * k : 4 * k + 4, WIDTH:]
            grads_out[k, 8:12, :] = sum_result[4 * k : 4 * k + 4, :]
            grads_out[k, 12:13, :] = small[k : k + 1, :]


def split_kernel(
    grads, mid_out, feat_out, bias_out, slice_out, heat_out, ask_out, look_out, content_out,
    result_out, small,
):
    for k in range(32):
        mid_out[4 * k : 4 * k + 4, :] = grads[k, 0:4, :]
        feat_out[4 * k : 4 * k + 4, :] = grads[k, 4:8, :]
        result_out[4 * k : 4 * k + 4, :] = grads[k, 8:12, :]
        small[k : k + 1, :] = grads[k, 12:13, :]
    ask_out[...] = small[:D, 0:D]
    look_out[...] = small[:D, D : 2 * D]
    content_out[...] = small[:D, 2 * D : 3 * D]
    slice_out[...] = small[:D, 64 : 64 + SLICES]
    bias_out[...] = small[D : D + 1, :]
    heat_out[...] = small[D + 1 : D + 2, :HEADS]


def exchange(block, axes, copies):
    sent = jnp.broadcast_to(block[None], (copies,) + block.shape)
    return lax.all_to_all(sent, axes, 0, 0, tiled=True)


def sum_over_nodes(sent):
    part = jnp.sum(lax.all_to_all(sent, ("zh", "core"), 0, 0, tiled=True), 0)
    part = jnp.sum(exchange(part, ("y", "x"), 16), 0)
    return lax.all_gather(part, "core", axis=0, tiled=False)


def sum_over_all(sent):
    part = jnp.sum(lax.all_to_all(sent, PLANE, 0, 0, tiled=True), 0)
    part = jnp.sum(exchange(part, COLUMN, 16), 0)
    return exchange(part, PLANE, 32)


def whole(shape):
    return pl.BlockSpec(shape, lambda i: (0,) * len(shape))


def tiled(width):
    return pl.BlockSpec((TILE, width), lambda i: (i, 0))


def shape(dims, dtype=F32):
    return jax.ShapeDtypeStruct(dims, dtype)


def pool(x, g, hidden, aggregate, offset, assign, sharp, result):
    nodes = x.shape[0]
    return pl.pallas_call(
        pool_kernel,
        grid=(nodes // TILE,),
        in_specs=[
            pl.BlockSpec(memory_space=pltpu.SMEM),
            tiled(WIDTH), tiled(WIDTH), whole((WIDTH, WIDTH)), whole((WIDTH, WIDTH)),
            whole((1, WIDTH)), whole((D, SLICES)), whole((WIDTH, WIDTH)),
        ],
        out_specs=[tiled(LANES), tiled(3 * WIDTH), whole((4, SLICES + 1, 128))],
        out_shape=[
            shape((nodes, LANES)), shape((nodes, 3 * WIDTH), BF16), shape((4, SLICES + 1, 128)),
        ],
        scratch_shapes=[
            pltpu.VMEM((WIDTH, LANES), BF16), pltpu.VMEM((WIDTH, LANES), BF16),
            pltpu.VMEM((1, LANES), F32), pltpu.VMEM((LANES, LANES), BF16),
            pltpu.VMEM((LANES, LANES), F32), pltpu.VMEM((8, LANES), F32),
        ],
        compiler_params=pltpu.CompilerParams(vmem_limit_bytes=48 << 20),
        name="pool",
    )(sharp, x, g, hidden, aggregate, offset, assign, result)


def back(pool_sum, x, g, hidden, aggregate, assign, sharp, ask, look, content, probs, rows):
    nodes = x.shape[0]
    return pl.pallas_call(
        back_kernel,
        grid=(nodes // TILE,),
        in_specs=[
            pl.BlockSpec(memory_space=pltpu.SMEM), whole((2, SLICES + 1, 128)),
            whole((WIDTH, WIDTH)), whole((WIDTH, WIDTH)), whole((D, SLICES)),
            whole((D, D)), whole((D, D)), whole((D, D)),
            tiled(WIDTH), tiled(WIDTH), tiled(LANES), tiled(3 * WIDTH),
        ],
        out_specs=[tiled(WIDTH), whole((32, 13, 128))],
        out_shape=[shape((nodes, WIDTH)), shape((32, 13, 128))],
        scratch_shapes=[
            pltpu.VMEM((WIDTH, LANES), BF16), pltpu.VMEM((WIDTH, LANES), BF16),
            pltpu.VMEM((1, LANES), F32), pltpu.VMEM((LANES, LANES), BF16),
            pltpu.VMEM((LANES, LANES), BF16), pltpu.VMEM((1, LANES), F32),
            pltpu.VMEM((32, 128), F32), pltpu.VMEM((WIDTH, LANES), F32),
            pltpu.VMEM((WIDTH, WIDTH), F32), pltpu.VMEM((WIDTH, LANES), F32),
            pltpu.VMEM((8, WIDTH), F32), pltpu.VMEM((8, LANES), F32),
        ],
        compiler_params=pltpu.CompilerParams(vmem_limit_bytes=48 << 20),
        name="back",
    )(sharp, pool_sum, hidden, aggregate, assign, ask, look, content, x, g, probs, rows)


def split(grads):
    square = (WIDTH, WIDTH)
    outs = [
        square, square, (1, WIDTH), (D, SLICES), (1, HEADS), (D, D), (D, D), (D, D), square,
    ]
    return pl.pallas_call(
        split_kernel,
        out_shape=[shape(s) for s in outs],
        scratch_shapes=[pltpu.VMEM((32, 128), F32)],
        name="split",
    )(grads)


def shards(
    vertex_embedding_array,
    result_sensitivity,
    hidden_projection,
    aggregate_projection,
    aggregate_offset,
    assignment_projection,
    softmax_sharpness,
    state_asking_map,
    state_lookup_map,
    state_content_map,
    result_projection,
):
    x = vertex_embedding_array[0]
    g = result_sensitivity[0]
    probs, rows, pooled = pool(
        x, g, hidden_projection, aggregate_projection, aggregate_offset[None],
        assignment_projection, softmax_sharpness, result_projection,
    )
    pool_sum = sum_over_nodes(pooled)
    sense, grads = back(
        pool_sum, x, g, hidden_projection, aggregate_projection, assignment_projection,
        softmax_sharpness, state_asking_map, state_lookup_map, state_content_map, probs, rows,
    )
    mid, feat, bias, slices, heat, ask, look, content, result = split(sum_over_all(grads))
    return sense[None], mid, feat, bias[0], slices, heat[0], ask, look, content, result


def solution(mesh):
    fine = Mesh(mesh.devices.reshape(8, 4, 2, 4, 2), ("zl",) + NODE)
    nodes = P("zl", NODE, None)
    return jax.shard_map(
        shards,
        mesh=fine,
        in_specs=(nodes, nodes) + (P(),) * 9,
        out_specs=(nodes,) + (P(),) * 9,
        check_vma=False,
    )
```

```python
import jax
import jax.numpy as jnp
from jax import lax
from jax.experimental import pallas as pl
from jax.experimental.pallas import tpu as pltpu
from jax.sharding import Mesh, PartitionSpec as P

HEADS = 8
SLICES = 32
D = 16
WIDTH = HEADS * D
LANES = HEADS * SLICES
EPS = 1e-05
TILE = 2048
MEMBER = ("z4", "z2", "z1")
NODE = ("y", "zh", "x", "core")
BLOCK = ("z1", "y", "x", "core")
COLUMN = ("z4", "z2", "zh")
F32 = jnp.float32
BF16 = jnp.bfloat16


def dot(a, b, ca=1, cb=0):
    return lax.dot_general(
        a, b, (((ca,), (cb,)), ((), ())), preferred_element_type=F32
    )


def grid_of(shape):
    return lax.broadcasted_iota(jnp.int32, shape, 0), lax.broadcasted_iota(jnp.int32, shape, 1)


def match(shape, f, g):
    r, c = grid_of(shape)
    return f(r) == g(c)


def head16(i):
    return i >> 4


def in16(i):
    return i & 15


def lane_head(i):
    return i & 7


def lane_slice(i):
    return i >> 3


def same(i):
    return i


def block_slices(a16x32):
    rows = dot(match((WIDTH, D), in16, same).astype(BF16), a16x32).astype(BF16)
    wide = dot(rows, match((SLICES, LANES), same, lane_slice).astype(BF16))
    return jnp.where(match((WIDTH, LANES), head16, lane_head), wide, 0.0)


def block_square(a16x16):
    rows = dot(match((WIDTH, D), in16, same).astype(BF16), a16x16).astype(BF16)
    wide = dot(rows, match((D, WIDTH), same, in16).astype(BF16))
    return jnp.where(match((WIDTH, WIDTH), head16, head16), wide, 0.0)


def sharpness_row(sharp):
    col = lax.broadcasted_iota(jnp.int32, (1, LANES), 1) & 7
    row = jnp.zeros((1, LANES), F32)
    for h in range(HEADS):
        row = jnp.where(col == h, sharp[:, h : h + 1], row)
    return 1.0 / row


def parts(a):
    high = a.astype(BF16)
    return high, (a - high.astype(F32)).astype(BF16)


def head_sums():
    row, col = grid_of((2 * WIDTH, WIDTH))
    return ((row & 7) == (col & 7)).astype(BF16)


def group_sum(a, ones):
    high, low = parts(a[:, :WIDTH] + a[:, WIDTH:])
    return dot(jnp.concatenate([high, low], 1), ones)


def both_halves(a):
    return jnp.concatenate([a, a], 1)


def dot_left(a, b, cb=0):
    high, low = parts(a)
    return dot(jnp.concatenate([high, low], 1), jnp.concatenate([b, b], cb), 1, cb)


def dot_both(a, b, ca=1, cb=0):
    a_high, a_low = parts(a)
    b_high, b_low = parts(b)
    left = jnp.concatenate([a_high, a_high, a_low], ca)
    right = jnp.concatenate([b_high, b_low, b_high], cb)
    return dot(left, right, ca, cb)


def fold_lanes(a):
    for width in (64, 32, 16):
        a = a + pltpu.roll(a, width, 1)
    return a


def fold_rows(a, rows):
    return jnp.sum(a.reshape(a.shape[0] // rows, rows, a.shape[1]), 0)


def stack_heads(a):
    tall = jnp.broadcast_to(a[:, None, :], (SLICES, HEADS, WIDTH)).reshape(LANES, WIDTH)
    return jnp.where(match((LANES, WIDTH), lane_head, head16), tall, 0.0)


def unstack_heads(a):
    return jnp.sum(a.reshape(SLICES, HEADS, a.shape[1]), 1)


def pool_kernel(
    sharp, x, g, hidden, aggregate, offset, assign, result, rows_out, pool_out,
    weights, assign_wide, scale, ones, pooled, mass,
):
    step = pl.program_id(0)

    @pl.when(step == 0)
    def _():
        weights[:, :WIDTH] = hidden[...]
        weights[:, WIDTH:] = aggregate[...]
        assign_wide[...] = block_slices(assign[...]).astype(BF16)
        scale[...] = sharpness_row(sharp[...])
        ones[...] = head_sums()
        pooled[...] = jnp.zeros_like(pooled)
        mass[...] = jnp.zeros_like(mass)

    both = dot(x[...], weights[...])
    mid = both[:, :WIDTH].astype(BF16)
    feat = (both[:, WIDTH:] + offset[...]).astype(BF16)
    back = dot(g[...], result[...], 1, 1).astype(BF16)
    rows_out[:, :WIDTH] = mid
    rows_out[:, WIDTH : 2 * WIDTH] = back
    rows_out[:, 2 * WIDTH :] = feat
    expon = jnp.exp(dot(mid, assign_wide[...]) * scale[...])
    probs = expon * both_halves(1.0 / group_sum(expon, ones[...]))
    mass[...] += fold_rows(probs, 8)
    pooled[...] += dot(probs.astype(BF16), jnp.concatenate([back, feat], 1), 0, 0)

    @pl.when(step == pl.num_programs(0) - 1)
    def _():
        row, col = grid_of((LANES, LANES))
        small = unstack_heads(jnp.where((row & 7) == ((col & 127) >> 4), pooled[...], 0.0))
        total = jnp.sum(mass[...], 0, keepdims=True)
        for z in range(2):
            pool_out[2 * z, :SLICES] = small[:, WIDTH:]
            pool_out[2 * z, SLICES:] = total[:, :WIDTH]
            pool_out[2 * z + 1, :SLICES] = small[:, :WIDTH]
            pool_out[2 * z + 1, SLICES:] = total[:, WIDTH:]


def attend_terms(pool, ask, look, content, ones):
    numer = pool[0, :SLICES]
    token_grad = pool[1, :SLICES]
    mass = jnp.concatenate([pool[0, SLICES:], pool[1, SLICES:]], 1)
    spread = jnp.where(match((SLICES, LANES), same, lane_slice), mass, 0.0)
    heads = match((LANES, WIDTH), lane_head, head16)
    heads_half = heads.astype(BF16)
    high, low = parts(spread)
    rest = (spread - high.astype(F32) - low.astype(F32)).astype(BF16)
    denom = dot(jnp.concatenate([high, low, rest], 1), jnp.concatenate([heads_half] * 3, 0)) + EPS
    inverse = 1.0 / denom
    tokens = numer * inverse
    maps = jnp.concatenate([block_square(m[...]) for m in (ask, look, content)], 1).astype(BF16)
    q_k_v = dot_left(tokens, maps)
    q = q_k_v[:, :WIDTH]
    keys = stack_heads(q_k_v[:, WIDTH : 2 * WIDTH])
    values = stack_heads(q_k_v[:, 2 * WIDTH :])
    expon = jnp.exp(dot_both(q, keys, 1, 1) * 0.25)
    rows_back = dot_both(token_grad, values, 1, 1)
    rows = expon * both_halves(1.0 / group_sum(expon, ones))
    token_out = dot_both(rows, values)
    centre = both_halves(group_sum(rows_back * rows, ones))
    scores_back = rows * (rows_back - centre) * 0.25
    q_back = dot_both(scores_back, keys)
    k_back = unstack_heads(jnp.where(heads, dot_both(scores_back, q, 0, 0), 0.0))
    v_back = unstack_heads(jnp.where(heads, dot_both(rows, token_grad, 0, 0), 0.0))
    three = jnp.concatenate([q_back, k_back, v_back], 1)
    tok_back = dot_left(three, maps, 1)
    numer_back = tok_back * inverse
    folded = dot_left(numer_back * tokens, heads_half, 1)
    folded = jnp.where(match((SLICES, LANES), same, lane_slice), folded, 0.0)
    denom_back = -jnp.sum(folded, 0, keepdims=True)
    row, col = grid_of((WIDTH, 3 * WIDTH))
    wide = jnp.where((row >> 4) == ((col & 127) >> 4), dot_both(tokens, three, 0, 0), 0.0)
    wide = fold_rows(wide, D)
    grads = [fold_lanes(wide[:, i * WIDTH : (i + 1) * WIDTH]) for i in range(3)]
    return token_out, numer_back, denom_back, grads


def back_kernel(
    sharp, pool, hidden, aggregate, assign, ask, look, content, x, g, rows_in,
    sense_out, grads_out,
    weights, assign_wide, scale, ones, token_wide, denom_back, small,
    sum_pair, sum_slice, sum_bias, sum_heat,
):
    step = pl.program_id(0)

    @pl.when(step == 0)
    def _():
        weights[:, :WIDTH] = hidden[...]
        weights[:, WIDTH:] = aggregate[...]
        assign_wide[...] = block_slices(assign[...]).astype(BF16)
        scale[...] = sharpness_row(sharp[...])
        ones[...] = head_sums()
        token_out, numer_back, shift, grads = attend_terms(pool, ask, look, content, ones[...])
        token_wide[:, :WIDTH] = stack_heads(token_out).astype(BF16)
        token_wide[:, WIDTH:] = stack_heads(numer_back).astype(BF16)
        denom_back[...] = shift
        small[...] = jnp.zeros_like(small)
        lane = lax.broadcasted_iota(jnp.int32, (D, WIDTH), 1)
        for i, term in enumerate(grads):
            small[:D, :] += jnp.where((lane >> 4) == i, term, 0.0) * (1.0 / 64.0)
        for ref in (sum_pair, sum_slice, sum_bias, sum_heat):
            ref[...] = jnp.zeros_like(ref)

    mid = rows_in[:, :WIDTH]
    logits = dot(mid, assign_wide[...]) * scale[...]
    expon = jnp.exp(logits)
    probs = expon * both_halves(1.0 / group_sum(expon, ones[...]))
    prob_back = dot(rows_in[:, WIDTH:], token_wide[...], 1, 1) + denom_back[...]
    inner = both_halves(group_sum(probs * prob_back, ones[...]))
    logit_back = probs * (prob_back - inner)
    sum_heat[...] += fold_rows(logit_back * logits, 8)
    score_back = (logit_back * scale[...]).astype(BF16)
    mid_back = dot(score_back, assign_wide[...], 1, 1).astype(BF16)
    spread = dot(probs.astype(BF16), token_wide[...])
    mixed = spread[:, :WIDTH].astype(BF16)
    feat_wide = spread[:, WIDTH:]
    feat_back = feat_wide.astype(BF16)
    sum_bias[...] += fold_rows(feat_wide, 8)
    sense_out[...] = dot(jnp.concatenate([mid_back, feat_back], 1), weights[...], 1, 1)
    sum_slice[...] += dot(jnp.concatenate([x[...], mid], 1), score_back, 0, 0)
    sum_pair[...] += dot(
        jnp.concatenate([x[...], mixed], 1), jnp.concatenate([feat_back, g[...]], 1), 0, 0
    )

    @pl.when(step == pl.num_programs(0) - 1)
    def _():
        mid_grad = dot_left(sum_slice[:WIDTH], assign_wide[...], 1)
        kept = jnp.where(match((WIDTH, LANES), head16, lane_head), sum_slice[WIDTH:], 0.0)
        row, col = grid_of((LANES, WIDTH))
        kept = dot_left(fold_rows(kept, D), ((row >> 3) + 64 == col).astype(BF16))
        small[:D, :] += kept
        small[D : D + 1, :] = jnp.sum(sum_bias[...], 0, keepdims=True)
        heat = jnp.sum(sum_heat[...], 0, keepdims=True) * scale[...]
        heat = jnp.broadcast_to(heat[:, :WIDTH] + heat[:, WIDTH:], (8, WIDTH))
        for width in (64, 32, 16, 8):
            heat = heat + pltpu.roll(heat, width, 1)
        small[D + 1 : D + 2, :] = -heat[:1]
        sum_slice[:WIDTH, :WIDTH] = mid_grad
        for k in range(64):
            two = slice(2 * k, 2 * k + 2)
            low = slice(WIDTH + 2 * k, WIDTH + 2 * k + 2)
            grads_out[k, 0:2, :] = sum_slice[two, :WIDTH]
            grads_out[k, 2:4, :] = sum_pair[two, :WIDTH]
            grads_out[k, 4:6, :] = sum_pair[low, WIDTH:]
            grads_out[k, 6:8, :] = small[two, :]


def split_kernel(
    grads, mid_out, feat_out, bias_out, slice_out, heat_out, ask_out, look_out, content_out,
    result_out, small,
):
    for k in range(64):
        two = slice(2 * k, 2 * k + 2)
        mid_out[two, :] = grads[k, 0:2, :]
        feat_out[two, :] = grads[k, 2:4, :]
        result_out[two, :] = grads[k, 4:6, :]
        if k < 9:
            small[two, :] = grads[k, 6:8, :]
    ask_out[...] = small[:D, 0:D]
    look_out[...] = small[:D, D : 2 * D]
    content_out[...] = small[:D, 2 * D : 3 * D]
    slice_out[...] = small[:D, 64 : 64 + SLICES]
    bias_out[...] = small[D : D + 1, :]
    heat_out[...] = small[D + 1 : D + 2, :HEADS]


def exchange(block, axes, copies):
    sent = jnp.broadcast_to(block[None], (copies,) + block.shape)
    return lax.all_to_all(sent, axes, 0, 0, tiled=True)


def sum_over_nodes(sent):
    part = jnp.sum(lax.all_to_all(sent, ("zh", "core"), 0, 0, tiled=True), 0)
    part = jnp.sum(exchange(part, ("y", "x"), 16), 0)
    return lax.all_gather(part, "core", axis=0, tiled=False)


def sum_over_all(sent):
    part = jnp.sum(lax.all_to_all(sent, BLOCK, 0, 0, tiled=True), 0)
    part = jnp.sum(exchange(part, COLUMN, 8), 0)
    return exchange(part, BLOCK, 64)


def whole(shape):
    return pl.BlockSpec(shape, lambda i: (0,) * len(shape))


def tiled(width):
    return pl.BlockSpec((TILE, width), lambda i: (i, 0))


def hbm(a):
    return pltpu.with_memory_space_constraint(a, pltpu.HBM)


def shape(dims, dtype=F32):
    return jax.ShapeDtypeStruct(dims, dtype)


def pool(x, g, hidden, aggregate, offset, assign, sharp, result):
    nodes = x.shape[0]
    return pl.pallas_call(
        pool_kernel,
        grid=(nodes // TILE,),
        in_specs=[
            whole((1, HEADS)),
            tiled(WIDTH), tiled(WIDTH), whole((WIDTH, WIDTH)), whole((WIDTH, WIDTH)),
            whole((1, WIDTH)), whole((D, SLICES)), whole((WIDTH, WIDTH)),
        ],
        out_specs=[tiled(3 * WIDTH), whole((4, SLICES + 1, 128))],
        out_shape=[
            shape((nodes, 3 * WIDTH), BF16), shape((4, SLICES + 1, 128)),
        ],
        scratch_shapes=[
            pltpu.VMEM((WIDTH, LANES), BF16), pltpu.VMEM((WIDTH, LANES), BF16),
            pltpu.VMEM((1, LANES), F32), pltpu.VMEM((LANES, WIDTH), BF16),
            pltpu.VMEM((LANES, LANES), F32), pltpu.VMEM((8, LANES), F32),
        ],
        compiler_params=pltpu.CompilerParams(vmem_limit_bytes=40 << 20),
        name="pool",
    )(*[hbm(a) for a in (sharp, x, g, hidden, aggregate, offset, assign, result)])


def back(pool_sum, x, g, hidden, aggregate, assign, sharp, ask, look, content, rows):
    nodes = x.shape[0]
    return pl.pallas_call(
        back_kernel,
        grid=(nodes // TILE,),
        in_specs=[
            whole((1, HEADS)), whole((2, SLICES + 1, 128)),
            whole((WIDTH, WIDTH)), whole((WIDTH, WIDTH)), whole((D, SLICES)),
            whole((D, D)), whole((D, D)), whole((D, D)),
            tiled(WIDTH), tiled(WIDTH), tiled(3 * WIDTH),
        ],
        out_specs=[tiled(WIDTH), whole((64, 8, 128))],
        out_shape=[shape((nodes, WIDTH)), shape((64, 8, 128))],
        scratch_shapes=[
            pltpu.VMEM((WIDTH, LANES), BF16), pltpu.VMEM((WIDTH, LANES), BF16),
            pltpu.VMEM((1, LANES), F32), pltpu.VMEM((LANES, WIDTH), BF16),
            pltpu.VMEM((LANES, LANES), BF16), pltpu.VMEM((1, LANES), F32),
            pltpu.VMEM((WIDTH, WIDTH), F32), pltpu.VMEM((LANES, LANES), F32),
            pltpu.VMEM((LANES, LANES), F32),
            pltpu.VMEM((8, WIDTH), F32), pltpu.VMEM((8, LANES), F32),
        ],
        compiler_params=pltpu.CompilerParams(vmem_limit_bytes=40 << 20),
        name="back",
    )(hbm(sharp), pool_sum, *[hbm(a) for a in (hidden, aggregate, assign, ask, look, content, x, g)], rows)


def split(grads):
    square = (WIDTH, WIDTH)
    outs = [
        square, square, (1, WIDTH), (D, SLICES), (1, HEADS), (D, D), (D, D), (D, D), square,
    ]
    return pl.pallas_call(
        split_kernel,
        out_shape=[shape(s) for s in outs],
        scratch_shapes=[pltpu.VMEM((32, 128), F32)],
        name="split",
    )(grads)


def shards(
    vertex_embedding_array,
    result_sensitivity,
    hidden_projection,
    aggregate_projection,
    aggregate_offset,
    assignment_projection,
    softmax_sharpness,
    state_asking_map,
    state_lookup_map,
    state_content_map,
    result_projection,
):
    x = vertex_embedding_array[0]
    g = result_sensitivity[0]
    rows, pooled = pool(
        x, g, hidden_projection, aggregate_projection, aggregate_offset[None],
        assignment_projection, softmax_sharpness[None], result_projection,
    )
    pool_sum = sum_over_nodes(pooled)
    sense, grads = back(
        pool_sum, x, g, hidden_projection, aggregate_projection, assignment_projection,
        softmax_sharpness[None], state_asking_map, state_lookup_map, state_content_map, rows,
    )
    mid, feat, bias, slices, heat, ask, look, content, result = split(sum_over_all(grads))
    return sense[None], mid, feat, bias[0], slices, heat[0], ask, look, content, result


def solution(mesh):
    fine = Mesh(mesh.devices.reshape(2, 2, 2, 4, 2, 4, 2), MEMBER + NODE)
    nodes = P(MEMBER, NODE, None)
    return jax.shard_map(
        shards,
        mesh=fine,
        in_specs=(nodes, nodes) + (P(),) * 9,
        out_specs=(nodes,) + (P(),) * 9,
        check_vma=False,
    )
```

```python
import jax
import jax.numpy as jnp
from jax import lax
from jax.experimental import pallas as pl
from jax.experimental.pallas import tpu as pltpu
from jax.sharding import Mesh, PartitionSpec as P

HEADS = 8
SLICES = 32
D = 16
WIDTH = HEADS * D
LANES = HEADS * SLICES
EPS = 1e-05
TILE = 2048
GRAD_ROWS = 512
MEMBER = ("z4", "z2", "z1")
NODE = ("y", "zh", "x", "core")
BLOCK = ("z1", "y", "x", "core")
COLUMN = ("z4", "z2", "zh")
F32 = jnp.float32
BF16 = jnp.bfloat16


def dot(a, b, ca=1, cb=0):
    return lax.dot_general(
        a, b, (((ca,), (cb,)), ((), ())), preferred_element_type=F32
    )


def grid_of(shape):
    return lax.broadcasted_iota(jnp.int32, shape, 0), lax.broadcasted_iota(jnp.int32, shape, 1)


def match(shape, f, g):
    r, c = grid_of(shape)
    return f(r) == g(c)


def head16(i):
    return i >> 4


def in16(i):
    return i & 15


def lane_head(i):
    return i & 7


def lane_slice(i):
    return i >> 3


def same(i):
    return i


def block_slices(a16x32):
    rows = dot(match((WIDTH, D), in16, same).astype(BF16), a16x32).astype(BF16)
    wide = dot(rows, match((SLICES, LANES), same, lane_slice).astype(BF16))
    return jnp.where(match((WIDTH, LANES), head16, lane_head), wide, 0.0)


def block_square(a16x16):
    rows = dot(match((WIDTH, D), in16, same).astype(BF16), a16x16).astype(BF16)
    wide = dot(rows, match((D, WIDTH), same, in16).astype(BF16))
    return jnp.where(match((WIDTH, WIDTH), head16, head16), wide, 0.0)


def sharpness_row(sharp):
    col = lax.broadcasted_iota(jnp.int32, (1, LANES), 1) & 7
    row = jnp.zeros((1, LANES), F32)
    for h in range(HEADS):
        row = jnp.where(col == h, sharp[:, h : h + 1], row)
    return 1.0 / row


def parts(a):
    high = a.astype(BF16)
    return high, (a - high.astype(F32)).astype(BF16)


def head_sums():
    row, col = grid_of((2 * WIDTH, WIDTH))
    return ((row & 7) == (col & 7)).astype(BF16)


def group_sum(a, ones):
    high, low = parts(a[:, :WIDTH] + a[:, WIDTH:])
    return dot(jnp.concatenate([high, low], 1), ones)


def both_halves(a):
    return jnp.concatenate([a, a], 1)


def dot_left(a, b, cb=0):
    high, low = parts(a)
    return dot(jnp.concatenate([high, low], 1), jnp.concatenate([b, b], cb), 1, cb)


def dot_both(a, b, ca=1, cb=0):
    a_high, a_low = parts(a)
    b_high, b_low = parts(b)
    left = jnp.concatenate([a_high, a_high, a_low], ca)
    right = jnp.concatenate([b_high, b_low, b_high], cb)
    return dot(left, right, ca, cb)


def fold_lanes(a):
    for width in (64, 32, 16):
        a = a + pltpu.roll(a, width, 1)
    return a


def fold_rows(a, rows):
    return jnp.sum(a.reshape(a.shape[0] // rows, rows, a.shape[1]), 0)


def stack_heads(a):
    tall = jnp.broadcast_to(a[:, None, :], (SLICES, HEADS, WIDTH)).reshape(LANES, WIDTH)
    return jnp.where(match((LANES, WIDTH), lane_head, head16), tall, 0.0)


def unstack_heads(a):
    return jnp.sum(a.reshape(SLICES, HEADS, a.shape[1]), 1)


def pool_kernel(
    sharp, x, g, hidden, aggregate, offset, assign, result, rows_out, pool_out,
    weights, assign_wide, scale, ones, pooled, mass,
):
    step = pl.program_id(0)

    @pl.when(step == 0)
    def _():
        weights[:, :WIDTH] = hidden[...]
        weights[:, WIDTH:] = aggregate[...]
        assign_wide[...] = block_slices(assign[...]).astype(BF16)
        scale[...] = sharpness_row(sharp[...])
        ones[...] = head_sums()
        pooled[...] = jnp.zeros_like(pooled)
        mass[...] = jnp.zeros_like(mass)

    both = dot(x[...], weights[...])
    mid = both[:, :WIDTH].astype(BF16)
    feat = (both[:, WIDTH:] + offset[...]).astype(BF16)
    back = dot(g[...], result[...], 1, 1).astype(BF16)
    rows_out[:, :WIDTH] = mid
    rows_out[:, WIDTH : 2 * WIDTH] = back
    rows_out[:, 2 * WIDTH :] = feat
    expon = jnp.exp(dot(mid, assign_wide[...]) * scale[...])
    probs = expon * both_halves(1.0 / group_sum(expon, ones[...]))
    mass[...] += fold_rows(probs, 8)
    pooled[...] += dot(probs.astype(BF16), jnp.concatenate([back, feat], 1), 0, 0)

    @pl.when(step == pl.num_programs(0) - 1)
    def _():
        row, col = grid_of((LANES, LANES))
        small = unstack_heads(jnp.where((row & 7) == ((col & 127) >> 4), pooled[...], 0.0))
        total = jnp.sum(mass[...], 0, keepdims=True)
        for z in range(2):
            pool_out[2 * z, :SLICES] = small[:, WIDTH:]
            pool_out[2 * z, SLICES:] = total[:, :WIDTH]
            pool_out[2 * z + 1, :SLICES] = small[:, :WIDTH]
            pool_out[2 * z + 1, SLICES:] = total[:, WIDTH:]


def cross_kernel(
    sharp, assign, x, g, rows_in, probs_out, cross_out, assign_wide, scale, ones, mass,
):
    step = pl.program_id(0)

    @pl.when(step == 0)
    def _():
        assign_wide[...] = block_slices(assign[...]).astype(BF16)
        scale[...] = sharpness_row(sharp[...])
        ones[...] = head_sums()
        cross_out[...] = jnp.zeros_like(cross_out)
        mass[...] = jnp.zeros_like(mass)

    expon = jnp.exp(dot(rows_in[:, :WIDTH], assign_wide[...]) * scale[...])
    probs = expon * both_halves(1.0 / group_sum(expon, ones[...]))
    probs_out[...] = probs
    half = probs.astype(BF16)
    mass[...] += fold_rows(half.astype(F32), 8)
    cross_out[:LANES] += dot(half, jnp.concatenate([x[...], g[...]], 1), 0, 0)

    @pl.when(step == pl.num_programs(0) - 1)
    def _():
        total = jnp.sum(mass[...], 0, keepdims=True)
        cross_out[LANES:] = jnp.broadcast_to(total, (8, LANES))


def attend_terms(pool, ask, look, content, ones):
    numer = pool[0, :SLICES]
    token_grad = pool[1, :SLICES]
    mass = jnp.concatenate([pool[0, SLICES:], pool[1, SLICES:]], 1)
    spread = jnp.where(match((SLICES, LANES), same, lane_slice), mass, 0.0)
    heads = match((LANES, WIDTH), lane_head, head16)
    heads_half = heads.astype(BF16)
    high, low = parts(spread)
    rest = (spread - high.astype(F32) - low.astype(F32)).astype(BF16)
    denom = dot(jnp.concatenate([high, low, rest], 1), jnp.concatenate([heads_half] * 3, 0)) + EPS
    inverse = 1.0 / denom
    tokens = numer * inverse
    maps = jnp.concatenate([block_square(m[...]) for m in (ask, look, content)], 1).astype(BF16)
    q_k_v = dot_left(tokens, maps)
    q = q_k_v[:, :WIDTH]
    keys = stack_heads(q_k_v[:, WIDTH : 2 * WIDTH])
    values = stack_heads(q_k_v[:, 2 * WIDTH :])
    expon = jnp.exp(dot_both(q, keys, 1, 1) * 0.25)
    rows_back = dot_both(token_grad, values, 1, 1)
    rows = expon * both_halves(1.0 / group_sum(expon, ones))
    token_out = dot_both(rows, values)
    centre = both_halves(group_sum(rows_back * rows, ones))
    scores_back = rows * (rows_back - centre) * 0.25
    q_back = dot_both(scores_back, keys)
    k_back = unstack_heads(jnp.where(heads, dot_both(scores_back, q, 0, 0), 0.0))
    v_back = unstack_heads(jnp.where(heads, dot_both(rows, token_grad, 0, 0), 0.0))
    three = jnp.concatenate([q_back, k_back, v_back], 1)
    tok_back = dot_left(three, maps, 1)
    numer_back = tok_back * inverse
    folded = dot_left(numer_back * tokens, heads_half, 1)
    folded = jnp.where(match((SLICES, LANES), same, lane_slice), folded, 0.0)
    denom_back = -jnp.sum(folded, 0, keepdims=True)
    row, col = grid_of((WIDTH, 3 * WIDTH))
    wide = jnp.where((row >> 4) == ((col & 127) >> 4), dot_both(tokens, three, 0, 0), 0.0)
    wide = fold_rows(wide, D)
    grads = [fold_lanes(wide[:, i * WIDTH : (i + 1) * WIDTH]) for i in range(3)]
    return token_out, numer_back, denom_back, grads


def back_kernel(
    sharp, assign, ask, look, content, pool, cross, rows_in, x_hbm, probs_hbm,
    score_hbm, numer_out, grads_out,
    x, probs_all, score_all, assign_wide, scale, ones, token_wide, denom_back, small, sum_slice, sum_heat,
    sems, out_sems,
):
    step = pl.program_id(0)
    last = pl.num_programs(0) - 1
    tiles = x.shape[0] // TILE

    def fetches(i):
        t = slice(i * TILE, (i + 1) * TILE)
        return [
            pltpu.make_async_copy(probs_hbm.at[t], probs_all.at[t], sems.at[2 * i]),
            pltpu.make_async_copy(x_hbm.at[t], x.at[t], sems.at[2 * i + 1]),
        ]

    @pl.when(step == 0)
    def _():
        for i in range(tiles):
            for copy in fetches(i):
                copy.start()
        assign_wide[...] = block_slices(assign[...]).astype(BF16)
        scale[...] = sharpness_row(sharp[...])
        ones[...] = head_sums()
        token_out, numer_back, shift, grads = attend_terms(pool, ask, look, content, ones[...])
        token_wide[:, :WIDTH] = stack_heads(token_out).astype(BF16)
        token_wide[:, WIDTH:] = stack_heads(numer_back).astype(BF16)
        denom_back[...] = shift
        small[...] = jnp.zeros_like(small)
        lane = lax.broadcasted_iota(jnp.int32, (D, WIDTH), 1)
        for i, term in enumerate(grads):
            small[:D, :] += jnp.where((lane >> 4) == i, term, 0.0) * (1.0 / 64.0)
        sum_slice[...] = jnp.zeros_like(sum_slice)
        sum_heat[...] = jnp.zeros_like(sum_heat)

    def sends(i):
        t = slice(i * TILE, (i + 1) * TILE)
        return pltpu.make_async_copy(score_all.at[t], score_hbm.at[t], out_sems.at[i])

    for i in range(tiles):

        @pl.when(step == i)
        def _(i=i):
            for copy in fetches(i):
                copy.wait()

    here = pl.ds(pl.multiple_of(step * TILE, TILE), TILE)
    mid = rows_in[:, :WIDTH]
    probs = probs_all[here]
    logits = dot(mid, assign_wide[...]) * scale[...]
    prob_back = dot(rows_in[:, WIDTH:], token_wide[...], 1, 1) + denom_back[...]
    inner = both_halves(group_sum(probs * prob_back, ones[...]))
    logit_back = probs * (prob_back - inner)
    sum_heat[...] += fold_rows(logit_back * logits, 8)
    score_back = (logit_back * scale[...]).astype(BF16)
    score_all[here] = score_back
    for i in range(tiles):

        @pl.when(step == i)
        def _(i=i):
            sends(i).start()

    sum_slice[...] += dot(jnp.concatenate([x[here], mid], 1), score_back, 0, 0)

    @pl.when(step == last)
    def _():
        mid_grad = dot_left(sum_slice[:WIDTH], assign_wide[...], 1)
        tokens = token_wide[:, :WIDTH]
        numers = token_wide[:, WIDTH:]
        cross_high, cross_low = parts(cross[:LANES])
        feat_grad = dot(cross_high[:, :WIDTH], numers, 0, 0) + dot(
            cross_low[:, :WIDTH], numers, 0, 0
        )
        result_grad = dot(tokens, cross_high[:, WIDTH:], 0, 0) + dot(
            tokens, cross_low[:, WIDTH:], 0, 0
        )
        mass_high, mass_low = parts(cross[LANES:])
        mass_rest = (
            cross[LANES:] - mass_high.astype(F32) - mass_low.astype(F32)
        ).astype(BF16)
        bias_grad = dot(mass_high, numers) + dot(mass_low, numers) + dot(mass_rest, numers)
        kept = jnp.where(match((WIDTH, LANES), head16, lane_head), sum_slice[WIDTH:], 0.0)
        row, col = grid_of((LANES, WIDTH))
        kept = dot_left(fold_rows(kept, D), ((row >> 3) + 64 == col).astype(BF16))
        small[:D, :] += kept
        small[D : D + 1, :] = bias_grad[:1]
        heat = jnp.sum(sum_heat[...], 0, keepdims=True) * scale[...]
        heat = jnp.broadcast_to(heat[:, :WIDTH] + heat[:, WIDTH:], (8, WIDTH))
        for width in (64, 32, 16, 8):
            heat = heat + pltpu.roll(heat, width, 1)
        small[D + 1 : D + 2, :] = -heat[:1]
        numer_out[...] = numers
        grads_out[:WIDTH] = mid_grad
        grads_out[WIDTH : 2 * WIDTH] = feat_grad
        grads_out[2 * WIDTH : 3 * WIDTH] = result_grad
        grads_out[3 * WIDTH :] = small[...]
        for i in range(tiles):
            sends(i).wait()


def sense_kernel(hidden, aggregate, assign, numers, score, probs, sense_out):
    weights = jnp.concatenate([hidden[...], aggregate[...]], 1)
    assign_wide = block_slices(assign[...]).astype(BF16)
    mid_back = dot(score[...], assign_wide, 1, 1).astype(BF16)
    feat_back = dot(probs[...].astype(BF16), numers[...]).astype(BF16)
    sense_out[...] = dot(jnp.concatenate([mid_back, feat_back], 1), weights, 1, 1)


def split_kernel(
    grads, mid_out, feat_out, bias_out, slice_out, heat_out, ask_out, look_out, content_out,
    result_out,
):
    mid_out[...] = grads[:WIDTH]
    feat_out[...] = grads[WIDTH : 2 * WIDTH]
    result_out[...] = grads[2 * WIDTH : 3 * WIDTH]
    small = grads[3 * WIDTH : 3 * WIDTH + 24]
    ask_out[...] = small[:D, 0:D]
    look_out[...] = small[:D, D : 2 * D]
    content_out[...] = small[:D, 2 * D : 3 * D]
    slice_out[...] = small[:D, 64 : 64 + SLICES]
    bias_out[...] = small[D : D + 1, :]
    heat_out[...] = small[D + 1 : D + 2, :HEADS]


def exchange(block, axes, copies):
    sent = jnp.broadcast_to(block[None], (copies,) + block.shape)
    return lax.all_to_all(sent, axes, 0, 0, tiled=True)


def sum_over_nodes(sent):
    part = jnp.sum(lax.all_to_all(sent, ("zh", "core"), 0, 0, tiled=True), 0)
    part = jnp.sum(exchange(part, ("y", "x"), 16), 0)
    return lax.all_gather(part, "core", axis=0, tiled=False)


def sum_over_all(sent):
    sent = sent.reshape(64, GRAD_ROWS // 64, 128)
    part = jnp.sum(lax.all_to_all(sent, BLOCK, 0, 0, tiled=True), 0)
    part = jnp.sum(exchange(part, COLUMN, 8), 0)
    return exchange(part, BLOCK, 64).reshape(GRAD_ROWS, 128)


def whole(shape):
    return pl.BlockSpec(shape, lambda i: (0,) * len(shape))


def tiled(width):
    return pl.BlockSpec((TILE, width), lambda i: (i, 0))


def hbm(a):
    return pltpu.with_memory_space_constraint(a, pltpu.HBM)


def shape(dims, dtype=F32):
    return jax.ShapeDtypeStruct(dims, dtype)


def pool(x, g, hidden, aggregate, offset, assign, sharp, result):
    nodes = x.shape[0]
    return pl.pallas_call(
        pool_kernel,
        grid=(nodes // TILE,),
        in_specs=[
            whole((1, HEADS)),
            tiled(WIDTH), tiled(WIDTH), whole((WIDTH, WIDTH)), whole((WIDTH, WIDTH)),
            whole((1, WIDTH)), whole((D, SLICES)), whole((WIDTH, WIDTH)),
        ],
        out_specs=[tiled(3 * WIDTH), whole((4, SLICES + 1, 128))],
        out_shape=[
            shape((nodes, 3 * WIDTH), BF16), shape((4, SLICES + 1, 128)),
        ],
        scratch_shapes=[
            pltpu.VMEM((WIDTH, LANES), BF16), pltpu.VMEM((WIDTH, LANES), BF16),
            pltpu.VMEM((1, LANES), F32), pltpu.VMEM((LANES, WIDTH), BF16),
            pltpu.VMEM((LANES, LANES), F32), pltpu.VMEM((8, LANES), F32),
        ],
        compiler_params=pltpu.CompilerParams(vmem_limit_bytes=40 << 20),
        name="pool",
    )(*[hbm(a) for a in (sharp, x, g, hidden, aggregate, offset, assign, result)])


def cross(x, g, assign, sharp, rows):
    nodes = x.shape[0]
    return pl.pallas_call(
        cross_kernel,
        grid=(nodes // TILE,),
        in_specs=[
            whole((1, HEADS)), whole((D, SLICES)), tiled(WIDTH), tiled(WIDTH), tiled(3 * WIDTH),
        ],
        out_specs=[tiled(LANES), whole((LANES + 8, LANES))],
        out_shape=[pltpu.HBM((nodes, LANES), F32), shape((LANES + 8, LANES))],
        scratch_shapes=[
            pltpu.VMEM((WIDTH, LANES), BF16), pltpu.VMEM((1, LANES), F32),
            pltpu.VMEM((LANES, WIDTH), BF16), pltpu.VMEM((8, LANES), F32),
        ],
        compiler_params=pltpu.CompilerParams(vmem_limit_bytes=40 << 20),
        name="cross",
    )(hbm(sharp), hbm(assign), hbm(x), hbm(g), rows)


def back(pool_sum, crossed, x, assign, sharp, ask, look, content, probs, rows):
    nodes = x.shape[0]
    return pl.pallas_call(
        back_kernel,
        grid=(nodes // TILE,),
        in_specs=[
            whole((1, HEADS)), whole((D, SLICES)), whole((D, D)), whole((D, D)), whole((D, D)),
            whole((2, SLICES + 1, 128)), whole((LANES + 8, LANES)), tiled(3 * WIDTH),
            pl.BlockSpec(memory_space=pltpu.HBM), pl.BlockSpec(memory_space=pltpu.HBM),
        ],
        out_specs=[
            pl.BlockSpec(memory_space=pltpu.HBM), whole((LANES, WIDTH)), whole((GRAD_ROWS, 128)),
        ],
        out_shape=[
            pltpu.HBM((nodes, LANES), BF16), shape((LANES, WIDTH), BF16), shape((GRAD_ROWS, 128)),
        ],
        scratch_shapes=[
            pltpu.VMEM((nodes, WIDTH), BF16), pltpu.VMEM((nodes, LANES), F32),
            pltpu.VMEM((nodes, LANES), BF16),
            pltpu.VMEM((WIDTH, LANES), BF16), pltpu.VMEM((1, LANES), F32),
            pltpu.VMEM((LANES, WIDTH), BF16), pltpu.VMEM((LANES, LANES), BF16),
            pltpu.VMEM((1, LANES), F32), pltpu.VMEM((WIDTH, WIDTH), F32),
            pltpu.VMEM((LANES, LANES), F32), pltpu.VMEM((8, LANES), F32),
            pltpu.SemaphoreType.DMA((2 * (nodes // TILE),)),
            pltpu.SemaphoreType.DMA((nodes // TILE,)),
        ],
        compiler_params=pltpu.CompilerParams(vmem_limit_bytes=40 << 20),
        name="back",
    )(sharp, assign, ask, look, content, pool_sum, crossed, rows, hbm(x), hbm(probs))


def sense(hidden, aggregate, assign, numers, score, probs):
    nodes = score.shape[0]
    square = whole((WIDTH, WIDTH))
    return pl.pallas_call(
        sense_kernel,
        grid=(nodes // TILE,),
        in_specs=[
            square, square, whole((D, SLICES)), whole((LANES, WIDTH)), tiled(LANES), tiled(LANES),
        ],
        out_specs=tiled(WIDTH),
        out_shape=pltpu.HBM((nodes, WIDTH), F32),
        compiler_params=pltpu.CompilerParams(vmem_limit_bytes=40 << 20),
        name="sense",
    )(*[hbm(a) for a in (hidden, aggregate, assign)], numers, hbm(score), hbm(probs))


def split(grads):
    square = (WIDTH, WIDTH)
    outs = [
        square, square, (1, WIDTH), (D, SLICES), (1, HEADS), (D, D), (D, D), (D, D), square,
    ]
    return pl.pallas_call(
        split_kernel,
        out_shape=[shape(s) for s in outs],
        name="split",
    )(pltpu.with_memory_space_constraint(grads, pltpu.VMEM))


def shards(
    vertex_embedding_array,
    result_sensitivity,
    hidden_projection,
    aggregate_projection,
    aggregate_offset,
    assignment_projection,
    softmax_sharpness,
    state_asking_map,
    state_lookup_map,
    state_content_map,
    result_projection,
):
    x = vertex_embedding_array[0]
    g = result_sensitivity[0]
    rows, pooled = pool(
        x, g, hidden_projection, aggregate_projection, aggregate_offset[None],
        assignment_projection, softmax_sharpness[None], result_projection,
    )
    sharp = softmax_sharpness[None]
    pool_sum = sum_over_nodes(pooled)
    probs, crossed = cross(x, g, assignment_projection, sharp, rows)
    score, numers, grads = back(
        pool_sum, crossed, x, assignment_projection, sharp, state_asking_map, state_lookup_map,
        state_content_map, probs, rows,
    )
    nodes_out = sense(
        hidden_projection, aggregate_projection, assignment_projection, numers, score, probs
    )
    mid, feat, bias, slices, heat, ask, look, content, result = split(sum_over_all(grads))
    return nodes_out[None], mid, feat, bias[0], slices, heat[0], ask, look, content, result


def solution(mesh):
    fine = Mesh(mesh.devices.reshape(2, 2, 2, 4, 2, 4, 2), MEMBER + NODE)
    nodes = P(MEMBER, NODE, None)
    return jax.shard_map(
        shards,
        mesh=fine,
        in_specs=(nodes, nodes) + (P(),) * 9,
        out_specs=(nodes,) + (P(),) * 9,
        check_vma=False,
    )
```

```python
import jax
import jax.numpy as jnp
from jax import lax
from jax.experimental import pallas as pl
from jax.experimental.pallas import tpu as pltpu
from jax.sharding import Mesh, PartitionSpec as P

HEADS = 8
SLICES = 32
D = 16
WIDTH = HEADS * D
LANES = HEADS * SLICES
EPS = 1e-05
TILE = 2048
GRAD_ROWS = 512
MEMBER = ("z4", "z2", "z1")
NODE = ("y", "zh", "x", "core")
BLOCK = ("z1", "y", "x", "core")
COLUMN = ("z4", "z2", "zh")
F32 = jnp.float32
BF16 = jnp.bfloat16


def dot(a, b, ca=1, cb=0):
    return lax.dot_general(
        a, b, (((ca,), (cb,)), ((), ())), preferred_element_type=F32
    )


def grid_of(shape):
    return lax.broadcasted_iota(jnp.int32, shape, 0), lax.broadcasted_iota(jnp.int32, shape, 1)


def match(shape, f, g):
    r, c = grid_of(shape)
    return f(r) == g(c)


def head16(i):
    return i >> 4


def in16(i):
    return i & 15


def lane_head(i):
    return i & 7


def lane_slice(i):
    return i >> 3


def same(i):
    return i


def block_slices(a16x32):
    rows = dot(match((WIDTH, D), in16, same).astype(BF16), a16x32).astype(BF16)
    wide = dot(rows, match((SLICES, LANES), same, lane_slice).astype(BF16))
    return jnp.where(match((WIDTH, LANES), head16, lane_head), wide, 0.0)


def block_square(a16x16):
    rows = dot(match((WIDTH, D), in16, same).astype(BF16), a16x16).astype(BF16)
    wide = dot(rows, match((D, WIDTH), same, in16).astype(BF16))
    return jnp.where(match((WIDTH, WIDTH), head16, head16), wide, 0.0)


def sharpness_row(sharp):
    col = lax.broadcasted_iota(jnp.int32, (1, LANES), 1) & 7
    row = jnp.zeros((1, LANES), F32)
    for h in range(HEADS):
        row = jnp.where(col == h, sharp[:, h : h + 1], row)
    return 1.0 / row


def parts(a):
    high = a.astype(BF16)
    return high, (a - high.astype(F32)).astype(BF16)


def head_sums():
    row, col = grid_of((2 * WIDTH, WIDTH))
    return ((row & 7) == (col & 7)).astype(BF16)


def group_sum(a, ones):
    high, low = parts(a[:, :WIDTH] + a[:, WIDTH:])
    return dot(jnp.concatenate([high, low], 1), ones)


def both_halves(a):
    return jnp.concatenate([a, a], 1)


def dot_left(a, b, cb=0):
    high, low = parts(a)
    return dot(jnp.concatenate([high, low], 1), jnp.concatenate([b, b], cb), 1, cb)


def dot_both(a, b, ca=1, cb=0):
    a_high, a_low = parts(a)
    b_high, b_low = parts(b)
    left = jnp.concatenate([a_high, a_high, a_low], ca)
    right = jnp.concatenate([b_high, b_low, b_high], cb)
    return dot(left, right, ca, cb)


def fold_lanes(a):
    for width in (64, 32, 16):
        a = a + pltpu.roll(a, width, 1)
    return a


def fold_rows(a, rows):
    return jnp.sum(a.reshape(a.shape[0] // rows, rows, a.shape[1]), 0)


def stack_heads(a):
    tall = jnp.broadcast_to(a[:, None, :], (SLICES, HEADS, WIDTH)).reshape(LANES, WIDTH)
    return jnp.where(match((LANES, WIDTH), lane_head, head16), tall, 0.0)


def unstack_heads(a):
    return jnp.sum(a.reshape(SLICES, HEADS, a.shape[1]), 1)


def pool_kernel(
    sharp, x, g, hidden, aggregate, offset, assign, result, rows_out, pool_out,
    weights, assign_wide, scale, ones, pooled, mass,
):
    step = pl.program_id(0)

    @pl.when(step == 0)
    def _():
        weights[:, :WIDTH] = hidden[...]
        weights[:, WIDTH:] = aggregate[...]
        assign_wide[...] = block_slices(assign[...]).astype(BF16)
        scale[...] = sharpness_row(sharp[...])
        ones[...] = head_sums()
        pooled[...] = jnp.zeros_like(pooled)
        mass[...] = jnp.zeros_like(mass)

    both = dot(x[...], weights[...])
    mid = both[:, :WIDTH].astype(BF16)
    feat = (both[:, WIDTH:] + offset[...]).astype(BF16)
    back = dot(g[...], result[...], 1, 1).astype(BF16)
    rows_out[:, :WIDTH] = mid
    rows_out[:, WIDTH : 2 * WIDTH] = back
    rows_out[:, 2 * WIDTH :] = feat
    expon = jnp.exp(dot(mid, assign_wide[...]) * scale[...])
    probs = expon * both_halves(1.0 / group_sum(expon, ones[...]))
    mass[...] += fold_rows(probs, 8)
    pooled[...] += dot(probs.astype(BF16), jnp.concatenate([back, feat], 1), 0, 0)

    @pl.when(step == pl.num_programs(0) - 1)
    def _():
        row, col = grid_of((LANES, LANES))
        small = unstack_heads(jnp.where((row & 7) == ((col & 127) >> 4), pooled[...], 0.0))
        total = jnp.sum(mass[...], 0, keepdims=True)
        for z in range(2):
            pool_out[2 * z, :SLICES] = small[:, WIDTH:]
            pool_out[2 * z, SLICES:] = total[:, :WIDTH]
            pool_out[2 * z + 1, :SLICES] = small[:, :WIDTH]
            pool_out[2 * z + 1, SLICES:] = total[:, WIDTH:]


def cross_kernel(
    sharp, assign, x, g, rows_in, probs_out, cross_out, assign_wide, scale, ones, mass,
):
    step = pl.program_id(0)

    @pl.when(step == 0)
    def _():
        assign_wide[...] = block_slices(assign[...]).astype(BF16)
        scale[...] = sharpness_row(sharp[...])
        ones[...] = head_sums()
        cross_out[...] = jnp.zeros_like(cross_out)
        mass[...] = jnp.zeros_like(mass)

    expon = jnp.exp(dot(rows_in[:, :WIDTH], assign_wide[...]) * scale[...])
    probs = expon * both_halves(1.0 / group_sum(expon, ones[...]))
    probs_out[...] = probs
    half = probs.astype(BF16)
    mass[...] += fold_rows(half.astype(F32), 8)
    cross_out[:LANES] += dot(half, jnp.concatenate([x[...], g[...]], 1), 0, 0)

    @pl.when(step == pl.num_programs(0) - 1)
    def _():
        total = jnp.sum(mass[...], 0, keepdims=True)
        cross_out[LANES:] = jnp.broadcast_to(total, (8, LANES))


def attend_terms(pool, ask, look, content, ones):
    numer = pool[0, :SLICES]
    token_grad = pool[1, :SLICES]
    mass = jnp.concatenate([pool[0, SLICES:], pool[1, SLICES:]], 1)
    spread = jnp.where(match((SLICES, LANES), same, lane_slice), mass, 0.0)
    heads = match((LANES, WIDTH), lane_head, head16)
    heads_half = heads.astype(BF16)
    high, low = parts(spread)
    rest = (spread - high.astype(F32) - low.astype(F32)).astype(BF16)
    denom = dot(jnp.concatenate([high, low, rest], 1), jnp.concatenate([heads_half] * 3, 0)) + EPS
    inverse = 1.0 / denom
    tokens = numer * inverse
    maps = jnp.concatenate([block_square(m[...]) for m in (ask, look, content)], 1).astype(BF16)
    q_k_v = dot_left(tokens, maps)
    q = q_k_v[:, :WIDTH]
    keys = stack_heads(q_k_v[:, WIDTH : 2 * WIDTH])
    values = stack_heads(q_k_v[:, 2 * WIDTH :])
    expon = jnp.exp(dot_both(q, keys, 1, 1) * 0.25)
    rows_back = dot_both(token_grad, values, 1, 1)
    rows = expon * both_halves(1.0 / group_sum(expon, ones))
    token_out = dot_both(rows, values)
    centre = both_halves(group_sum(rows_back * rows, ones))
    scores_back = rows * (rows_back - centre) * 0.25
    q_back = dot_both(scores_back, keys)
    k_back = unstack_heads(jnp.where(heads, dot_both(scores_back, q, 0, 0), 0.0))
    v_back = unstack_heads(jnp.where(heads, dot_both(rows, token_grad, 0, 0), 0.0))
    three = jnp.concatenate([q_back, k_back, v_back], 1)
    tok_back = dot_left(three, maps, 1)
    numer_back = tok_back * inverse
    folded = dot_left(numer_back * tokens, heads_half, 1)
    folded = jnp.where(match((SLICES, LANES), same, lane_slice), folded, 0.0)
    denom_back = -jnp.sum(folded, 0, keepdims=True)
    row, col = grid_of((WIDTH, 3 * WIDTH))
    wide = jnp.where((row >> 4) == ((col & 127) >> 4), dot_both(tokens, three, 0, 0), 0.0)
    wide = fold_rows(wide, D)
    grads = [fold_lanes(wide[:, i * WIDTH : (i + 1) * WIDTH]) for i in range(3)]
    return token_out, numer_back, denom_back, grads


def back_kernel(
    sharp, assign, ask, look, content, pool, cross, rows_in, x_hbm, probs_hbm,
    score_hbm, numer_out, grads_out,
    x, probs_all, score_all, assign_wide, scale, ones, token_wide, denom_back, small, sum_slice, sum_heat,
    sems, out_sems,
):
    step = pl.program_id(0)
    last = pl.num_programs(0) - 1
    tiles = x.shape[0] // TILE

    def fetches(i):
        t = slice(i * TILE, (i + 1) * TILE)
        return [
            pltpu.make_async_copy(probs_hbm.at[t], probs_all.at[t], sems.at[2 * i]),
            pltpu.make_async_copy(x_hbm.at[t], x.at[t], sems.at[2 * i + 1]),
        ]

    @pl.when(step == 0)
    def _():
        for i in range(tiles):
            for copy in fetches(i):
                copy.start()
        assign_wide[...] = block_slices(assign[...]).astype(BF16)
        scale[...] = sharpness_row(sharp[...])
        ones[...] = head_sums()
        token_out, numer_back, shift, grads = attend_terms(pool, ask, look, content, ones[...])
        token_wide[:, :WIDTH] = stack_heads(token_out).astype(BF16)
        token_wide[:, WIDTH:] = stack_heads(numer_back).astype(BF16)
        denom_back[...] = shift
        small[...] = jnp.zeros_like(small)
        lane = lax.broadcasted_iota(jnp.int32, (D, WIDTH), 1)
        for i, term in enumerate(grads):
            small[:D, :] += jnp.where((lane >> 4) == i, term, 0.0) * (1.0 / 64.0)
        sum_slice[...] = jnp.zeros_like(sum_slice)
        sum_heat[...] = jnp.zeros_like(sum_heat)

    def sends(i):
        t = slice(i * TILE, (i + 1) * TILE)
        return pltpu.make_async_copy(score_all.at[t], score_hbm.at[t], out_sems.at[i])

    for i in range(tiles):

        @pl.when(step == i)
        def _(i=i):
            for copy in fetches(i):
                copy.wait()

    here = pl.ds(pl.multiple_of(step * TILE, TILE), TILE)
    mid = rows_in[:, :WIDTH]
    probs = probs_all[here]
    logits = dot(mid, assign_wide[...]) * scale[...]
    prob_back = dot(rows_in[:, WIDTH:], token_wide[...], 1, 1) + denom_back[...]
    inner = both_halves(group_sum(probs * prob_back, ones[...]))
    logit_back = probs * (prob_back - inner)
    sum_heat[...] += fold_rows(logit_back * logits, 8)
    score_back = (logit_back * scale[...]).astype(BF16)
    score_all[here] = score_back
    for i in range(tiles):

        @pl.when(step == i)
        def _(i=i):
            sends(i).start()

    sum_slice[...] += dot(jnp.concatenate([x[here], mid], 1), score_back, 0, 0)

    @pl.when(step == last)
    def _():
        mid_grad = dot_left(sum_slice[:WIDTH], assign_wide[...], 1)
        tokens = token_wide[:, :WIDTH]
        numers = token_wide[:, WIDTH:]
        cross_high, cross_low = parts(cross[:LANES])
        feat_grad = dot(cross_high[:, :WIDTH], numers, 0, 0) + dot(
            cross_low[:, :WIDTH], numers, 0, 0
        )
        result_grad = dot(tokens, cross_high[:, WIDTH:], 0, 0) + dot(
            tokens, cross_low[:, WIDTH:], 0, 0
        )
        mass_high, mass_low = parts(cross[LANES:])
        mass_rest = (
            cross[LANES:] - mass_high.astype(F32) - mass_low.astype(F32)
        ).astype(BF16)
        bias_grad = dot(mass_high, numers) + dot(mass_low, numers) + dot(mass_rest, numers)
        kept = jnp.where(match((WIDTH, LANES), head16, lane_head), sum_slice[WIDTH:], 0.0)
        row, col = grid_of((LANES, WIDTH))
        kept = dot_left(fold_rows(kept, D), ((row >> 3) + 64 == col).astype(BF16))
        small[:D, :] += kept
        small[D : D + 1, :] = bias_grad[:1]
        heat = jnp.sum(sum_heat[...], 0, keepdims=True) * scale[...]
        heat = jnp.broadcast_to(heat[:, :WIDTH] + heat[:, WIDTH:], (8, WIDTH))
        for width in (64, 32, 16, 8):
            heat = heat + pltpu.roll(heat, width, 1)
        small[D + 1 : D + 2, :] = -heat[:1]
        numer_out[...] = numers
        grads_out[:WIDTH] = mid_grad
        grads_out[WIDTH : 2 * WIDTH] = feat_grad
        grads_out[2 * WIDTH : 3 * WIDTH] = result_grad
        grads_out[3 * WIDTH :] = small[...]
        for i in range(tiles):
            sends(i).wait()


def sense_kernel(hidden, aggregate, assign, numers, score, probs, sense_out):
    weights = jnp.concatenate([hidden[...], aggregate[...]], 1)
    assign_wide = block_slices(assign[...]).astype(BF16)
    mid_back = dot(score[...], assign_wide, 1, 1).astype(BF16)
    feat_back = dot(probs[...].astype(BF16), numers[...]).astype(BF16)
    sense_out[...] = dot(jnp.concatenate([mid_back, feat_back], 1), weights, 1, 1)


def split_kernel(
    grads, mid_out, feat_out, bias_out, slice_out, heat_out, ask_out, look_out, content_out,
    result_out,
):
    mid_out[...] = grads[:WIDTH]
    feat_out[...] = grads[WIDTH : 2 * WIDTH]
    result_out[...] = grads[2 * WIDTH : 3 * WIDTH]
    small = grads[3 * WIDTH : 3 * WIDTH + 24]
    ask_out[...] = small[:D, 0:D]
    look_out[...] = small[:D, D : 2 * D]
    content_out[...] = small[:D, 2 * D : 3 * D]
    slice_out[...] = small[:D, 64 : 64 + SLICES]
    bias_out[...] = small[D : D + 1, :]
    heat_out[...] = small[D + 1 : D + 2, :HEADS]


def exchange(block, axes, copies):
    sent = jnp.broadcast_to(block[None], (copies,) + block.shape)
    return lax.all_to_all(sent, axes, 0, 0, tiled=True)


def sum_over_nodes(sent, beside):
    part = jnp.sum(lax.all_to_all(sent, ("zh", "core"), 0, 0, tiled=True), 0)
    part, beside = lax.optimization_barrier((part, beside))
    part = jnp.sum(exchange(part, ("y", "x"), 16), 0)
    return lax.all_gather(part, "core", axis=0, tiled=False), beside


def scatter_sum(sent):
    sent = sent.reshape(64, GRAD_ROWS // 64, 128)
    return jnp.sum(lax.all_to_all(sent, BLOCK, 0, 0, tiled=True), 0)


def gather_sum(part, beside):
    part = jnp.sum(exchange(part, COLUMN, 8), 0)
    part, beside = lax.optimization_barrier((part, beside))
    return exchange(part, BLOCK, 64).reshape(GRAD_ROWS, 128), beside


def whole(shape):
    return pl.BlockSpec(shape, lambda i: (0,) * len(shape))


def tiled(width):
    return pl.BlockSpec((TILE, width), lambda i: (i, 0))


def hbm(a):
    return pltpu.with_memory_space_constraint(a, pltpu.HBM)


def shape(dims, dtype=F32):
    return jax.ShapeDtypeStruct(dims, dtype)


def pool(x, g, hidden, aggregate, offset, assign, sharp, result):
    nodes = x.shape[0]
    return pl.pallas_call(
        pool_kernel,
        grid=(nodes // TILE,),
        in_specs=[
            whole((1, HEADS)),
            tiled(WIDTH), tiled(WIDTH), whole((WIDTH, WIDTH)), whole((WIDTH, WIDTH)),
            whole((1, WIDTH)), whole((D, SLICES)), whole((WIDTH, WIDTH)),
        ],
        out_specs=[tiled(3 * WIDTH), whole((4, SLICES + 1, 128))],
        out_shape=[
            shape((nodes, 3 * WIDTH), BF16), shape((4, SLICES + 1, 128)),
        ],
        scratch_shapes=[
            pltpu.VMEM((WIDTH, LANES), BF16), pltpu.VMEM((WIDTH, LANES), BF16),
            pltpu.VMEM((1, LANES), F32), pltpu.VMEM((LANES, WIDTH), BF16),
            pltpu.VMEM((LANES, LANES), F32), pltpu.VMEM((8, LANES), F32),
        ],
        compiler_params=pltpu.CompilerParams(vmem_limit_bytes=40 << 20),
        name="pool",
    )(*[hbm(a) for a in (sharp, x, g, hidden, aggregate, offset, assign, result)])


def cross(x, g, assign, sharp, rows):
    nodes = x.shape[0]
    return pl.pallas_call(
        cross_kernel,
        grid=(nodes // TILE,),
        in_specs=[
            whole((1, HEADS)), whole((D, SLICES)), tiled(WIDTH), tiled(WIDTH), tiled(3 * WIDTH),
        ],
        out_specs=[tiled(LANES), whole((LANES + 8, LANES))],
        out_shape=[pltpu.HBM((nodes, LANES), F32), shape((LANES + 8, LANES))],
        scratch_shapes=[
            pltpu.VMEM((WIDTH, LANES), BF16), pltpu.VMEM((1, LANES), F32),
            pltpu.VMEM((LANES, WIDTH), BF16), pltpu.VMEM((8, LANES), F32),
        ],
        compiler_params=pltpu.CompilerParams(vmem_limit_bytes=40 << 20),
        name="cross",
    )(hbm(sharp), hbm(assign), hbm(x), hbm(g), rows)


def back(pool_sum, crossed, x, assign, sharp, ask, look, content, probs, rows):
    nodes = x.shape[0]
    return pl.pallas_call(
        back_kernel,
        grid=(nodes // TILE,),
        in_specs=[
            whole((1, HEADS)), whole((D, SLICES)), whole((D, D)), whole((D, D)), whole((D, D)),
            whole((2, SLICES + 1, 128)), whole((LANES + 8, LANES)), tiled(3 * WIDTH),
            pl.BlockSpec(memory_space=pltpu.HBM), pl.BlockSpec(memory_space=pltpu.HBM),
        ],
        out_specs=[
            pl.BlockSpec(memory_space=pltpu.HBM), whole((LANES, WIDTH)), whole((GRAD_ROWS, 128)),
        ],
        out_shape=[
            pltpu.HBM((nodes, LANES), BF16), shape((LANES, WIDTH), BF16), shape((GRAD_ROWS, 128)),
        ],
        scratch_shapes=[
            pltpu.VMEM((nodes, WIDTH), BF16), pltpu.VMEM((nodes, LANES), F32),
            pltpu.VMEM((nodes, LANES), BF16),
            pltpu.VMEM((WIDTH, LANES), BF16), pltpu.VMEM((1, LANES), F32),
            pltpu.VMEM((LANES, WIDTH), BF16), pltpu.VMEM((LANES, LANES), BF16),
            pltpu.VMEM((1, LANES), F32), pltpu.VMEM((WIDTH, WIDTH), F32),
            pltpu.VMEM((LANES, LANES), F32), pltpu.VMEM((8, LANES), F32),
            pltpu.SemaphoreType.DMA((2 * (nodes // TILE),)),
            pltpu.SemaphoreType.DMA((nodes // TILE,)),
        ],
        compiler_params=pltpu.CompilerParams(vmem_limit_bytes=40 << 20),
        name="back",
    )(sharp, assign, ask, look, content, pool_sum, crossed, rows, hbm(x), hbm(probs))


def sense(hidden, aggregate, assign, numers, score, probs):
    nodes = score.shape[0]
    square = whole((WIDTH, WIDTH))
    return pl.pallas_call(
        sense_kernel,
        grid=(nodes // TILE,),
        in_specs=[
            square, square, whole((D, SLICES)), whole((LANES, WIDTH)), tiled(LANES), tiled(LANES),
        ],
        out_specs=tiled(WIDTH),
        out_shape=pltpu.HBM((nodes, WIDTH), F32),
        compiler_params=pltpu.CompilerParams(vmem_limit_bytes=40 << 20),
        name="sense",
    )(*[hbm(a) for a in (hidden, aggregate, assign)], numers, hbm(score), hbm(probs))


def split(grads):
    square = (WIDTH, WIDTH)
    outs = [
        square, square, (1, WIDTH), (D, SLICES), (1, HEADS), (D, D), (D, D), (D, D), square,
    ]
    return pl.pallas_call(
        split_kernel,
        out_shape=[shape(s) for s in outs],
        name="split",
    )(pltpu.with_memory_space_constraint(grads, pltpu.VMEM))


def shards(
    vertex_embedding_array,
    result_sensitivity,
    hidden_projection,
    aggregate_projection,
    aggregate_offset,
    assignment_projection,
    softmax_sharpness,
    state_asking_map,
    state_lookup_map,
    state_content_map,
    result_projection,
):
    x = vertex_embedding_array[0]
    g = result_sensitivity[0]
    rows, pooled = pool(
        x, g, hidden_projection, aggregate_projection, aggregate_offset[None],
        assignment_projection, softmax_sharpness[None], result_projection,
    )
    sharp = softmax_sharpness[None]
    beside = cross(x, g, assignment_projection, sharp, rows)
    pool_sum, (probs, crossed) = sum_over_nodes(pooled, beside)
    score, numers, grads = back(
        pool_sum, crossed, x, assignment_projection, sharp, state_asking_map, state_lookup_map,
        state_content_map, probs, rows,
    )
    part, score = lax.optimization_barrier((scatter_sum(grads), score))
    nodes_out = sense(
        hidden_projection, aggregate_projection, assignment_projection, numers, score, probs
    )
    total, nodes_out = gather_sum(part, nodes_out)
    mid, feat, bias, slices, heat, ask, look, content, result = split(total)
    return nodes_out[None], mid, feat, bias[0], slices, heat[0], ask, look, content, result


def solution(mesh):
    fine = Mesh(mesh.devices.reshape(2, 2, 2, 4, 2, 4, 2), MEMBER + NODE)
    nodes = P(MEMBER, NODE, None)
    return jax.shard_map(
        shards,
        mesh=fine,
        in_specs=(nodes, nodes) + (P(),) * 9,
        out_specs=(nodes,) + (P(),) * 9,
        check_vma=False,
    )
```

```python
import jax
import jax.numpy as jnp
from jax import lax
from jax.experimental import pallas as pl
from jax.experimental.pallas import tpu as pltpu
from jax.sharding import Mesh, PartitionSpec as P

HEADS = 8
SLICES = 32
D = 16
WIDTH = HEADS * D
LANES = HEADS * SLICES
EPS = 1e-05
TILE = 2048
GRAD_ROWS = 512
MEMBER = ("z4", "z2", "z1")
NODE = ("y", "zh", "x", "core")
BLOCK = ("z1", "y", "x", "core")
COLUMN = ("z4", "z2", "zh")
F32 = jnp.float32
BF16 = jnp.bfloat16


def dot(a, b, ca=1, cb=0):
    return lax.dot_general(
        a, b, (((ca,), (cb,)), ((), ())), preferred_element_type=F32
    )


def grid_of(shape):
    return lax.broadcasted_iota(jnp.int32, shape, 0), lax.broadcasted_iota(jnp.int32, shape, 1)


def match(shape, f, g):
    r, c = grid_of(shape)
    return f(r) == g(c)


def head16(i):
    return i >> 4


def in16(i):
    return i & 15


def lane_head(i):
    return i & 7


def lane_slice(i):
    return i >> 3


def same(i):
    return i


def block_slices(a16x32):
    rows = dot(match((WIDTH, D), in16, same).astype(BF16), a16x32).astype(BF16)
    wide = dot(rows, match((SLICES, LANES), same, lane_slice).astype(BF16))
    return jnp.where(match((WIDTH, LANES), head16, lane_head), wide, 0.0)


def block_square(a16x16):
    rows = dot(match((WIDTH, D), in16, same).astype(BF16), a16x16).astype(BF16)
    wide = dot(rows, match((D, WIDTH), same, in16).astype(BF16))
    return jnp.where(match((WIDTH, WIDTH), head16, head16), wide, 0.0)


def sharpness_row(sharp):
    col = lax.broadcasted_iota(jnp.int32, (1, LANES), 1) & 7
    row = jnp.zeros((1, LANES), F32)
    for h in range(HEADS):
        row = jnp.where(col == h, sharp[:, h : h + 1], row)
    return 1.0 / row


def parts(a):
    high = a.astype(BF16)
    return high, (a - high.astype(F32)).astype(BF16)


def head_sums():
    row, col = grid_of((2 * WIDTH, WIDTH))
    return ((row & 7) == (col & 7)).astype(BF16)


def group_sum(a, ones):
    high, low = parts(a[:, :WIDTH] + a[:, WIDTH:])
    return dot(jnp.concatenate([high, low], 1), ones)


def both_halves(a):
    return jnp.concatenate([a, a], 1)


def dot_left(a, b, cb=0):
    high, low = parts(a)
    return dot(jnp.concatenate([high, low], 1), jnp.concatenate([b, b], cb), 1, cb)


def dot_both(a, b, ca=1, cb=0):
    a_high, a_low = parts(a)
    b_high, b_low = parts(b)
    left = jnp.concatenate([a_high, a_high, a_low], ca)
    right = jnp.concatenate([b_high, b_low, b_high], cb)
    return dot(left, right, ca, cb)


def fold_lanes(a):
    for width in (64, 32, 16):
        a = a + pltpu.roll(a, width, 1)
    return a


def fold_rows(a, rows):
    return jnp.sum(a.reshape(a.shape[0] // rows, rows, a.shape[1]), 0)


def stack_heads(a):
    tall = jnp.broadcast_to(a[:, None, :], (SLICES, HEADS, WIDTH)).reshape(LANES, WIDTH)
    return jnp.where(match((LANES, WIDTH), lane_head, head16), tall, 0.0)


def unstack_heads(a):
    return jnp.sum(a.reshape(SLICES, HEADS, a.shape[1]), 1)


def pool_kernel(
    sharp, x, g, hidden, aggregate, offset, assign, result, rows_out, pool_out,
    weights, assign_wide, scale, ones, pooled, mass,
):
    step = pl.program_id(0)

    @pl.when(step == 0)
    def _():
        weights[:, :WIDTH] = hidden[...]
        weights[:, WIDTH:] = aggregate[...]
        assign_wide[...] = block_slices(assign[...]).astype(BF16)
        scale[...] = sharpness_row(sharp[...])
        ones[...] = head_sums()
        pooled[...] = jnp.zeros_like(pooled)
        mass[...] = jnp.zeros_like(mass)

    both = dot(x[...], weights[...])
    mid = both[:, :WIDTH].astype(BF16)
    feat = (both[:, WIDTH:] + offset[...]).astype(BF16)
    back = dot(g[...], result[...], 1, 1).astype(BF16)
    rows_out[:, :WIDTH] = mid
    rows_out[:, WIDTH : 2 * WIDTH] = back
    rows_out[:, 2 * WIDTH :] = feat
    expon = jnp.exp(dot(mid, assign_wide[...]) * scale[...])
    probs = expon * both_halves(1.0 / group_sum(expon, ones[...]))
    mass[...] += fold_rows(probs, 8)
    pooled[...] += dot(probs.astype(BF16), jnp.concatenate([back, feat], 1), 0, 0)

    @pl.when(step == pl.num_programs(0) - 1)
    def _():
        row, col = grid_of((LANES, LANES))
        small = unstack_heads(jnp.where((row & 7) == ((col & 127) >> 4), pooled[...], 0.0))
        total = jnp.sum(mass[...], 0, keepdims=True)
        for z in range(2):
            pool_out[2 * z, :SLICES] = small[:, WIDTH:]
            pool_out[2 * z, SLICES:] = total[:, :WIDTH]
            pool_out[2 * z + 1, :SLICES] = small[:, :WIDTH]
            pool_out[2 * z + 1, SLICES:] = total[:, WIDTH:]


def cross_kernel(
    sharp, assign, rows_in, x_hbm, g_hbm, cross_out, probs_hbm,
    pairs, probs_all, assign_wide, scale, ones, mass, sems,
):
    step = pl.program_id(0)
    tiles = probs_hbm.shape[0] // TILE

    def moves(i):
        t = slice(i * TILE, (i + 1) * TILE)
        return (
            pltpu.make_async_copy(x_hbm.at[t], pairs.at[t, :WIDTH], sems.at[3 * i]),
            pltpu.make_async_copy(g_hbm.at[t], pairs.at[t, WIDTH:], sems.at[3 * i + 1]),
            pltpu.make_async_copy(probs_all.at[t], probs_hbm.at[t], sems.at[3 * i + 2]),
        )

    @pl.when(step == 0)
    def _():
        for i in range(tiles):
            for copy in moves(i)[:2]:
                copy.start()
        assign_wide[...] = block_slices(assign[...]).astype(BF16)
        scale[...] = sharpness_row(sharp[...])
        ones[...] = head_sums()
        cross_out[...] = jnp.zeros_like(cross_out)
        mass[...] = jnp.zeros_like(mass)

    here = pl.ds(pl.multiple_of(step * TILE, TILE), TILE)
    expon = jnp.exp(dot(rows_in[:, :WIDTH], assign_wide[...]) * scale[...])
    probs = expon * both_halves(1.0 / group_sum(expon, ones[...]))
    probs_all[here] = probs
    for i in range(tiles):

        @pl.when(step == i)
        def _(i=i):
            moves(i)[2].start()
            for copy in moves(i)[:2]:
                copy.wait()

    half = probs.astype(BF16)
    mass[...] += fold_rows(half.astype(F32), 8)
    cross_out[:LANES] += dot(half, pairs[here], 0, 0)

    @pl.when(step == tiles - 1)
    def _():
        total = jnp.sum(mass[...], 0, keepdims=True)
        cross_out[LANES:] = jnp.broadcast_to(total, (8, LANES))
        for i in range(tiles):
            moves(i)[2].wait()


def attend_terms(pool, ask, look, content, ones):
    numer = pool[0, :SLICES]
    token_grad = pool[1, :SLICES]
    mass = jnp.concatenate([pool[0, SLICES:], pool[1, SLICES:]], 1)
    spread = jnp.where(match((SLICES, LANES), same, lane_slice), mass, 0.0)
    heads = match((LANES, WIDTH), lane_head, head16)
    heads_half = heads.astype(BF16)
    high, low = parts(spread)
    rest = (spread - high.astype(F32) - low.astype(F32)).astype(BF16)
    denom = dot(jnp.concatenate([high, low, rest], 1), jnp.concatenate([heads_half] * 3, 0)) + EPS
    inverse = 1.0 / denom
    tokens = numer * inverse
    maps = jnp.concatenate([block_square(m[...]) for m in (ask, look, content)], 1).astype(BF16)
    q_k_v = dot_left(tokens, maps)
    q = q_k_v[:, :WIDTH]
    keys = stack_heads(q_k_v[:, WIDTH : 2 * WIDTH])
    values = stack_heads(q_k_v[:, 2 * WIDTH :])
    expon = jnp.exp(dot_both(q, keys, 1, 1) * 0.25)
    rows_back = dot_both(token_grad, values, 1, 1)
    rows = expon * both_halves(1.0 / group_sum(expon, ones))
    token_out = dot_both(rows, values)
    centre = both_halves(group_sum(rows_back * rows, ones))
    scores_back = rows * (rows_back - centre) * 0.25
    q_back = dot_both(scores_back, keys)
    k_back = unstack_heads(jnp.where(heads, dot_both(scores_back, q, 0, 0), 0.0))
    v_back = unstack_heads(jnp.where(heads, dot_both(rows, token_grad, 0, 0), 0.0))
    three = jnp.concatenate([q_back, k_back, v_back], 1)
    tok_back = dot_left(three, maps, 1)
    numer_back = tok_back * inverse
    folded = dot_left(numer_back * tokens, heads_half, 1)
    folded = jnp.where(match((SLICES, LANES), same, lane_slice), folded, 0.0)
    denom_back = -jnp.sum(folded, 0, keepdims=True)
    row, col = grid_of((WIDTH, 3 * WIDTH))
    wide = jnp.where((row >> 4) == ((col & 127) >> 4), dot_both(tokens, three, 0, 0), 0.0)
    wide = fold_rows(wide, D)
    grads = [fold_lanes(wide[:, i * WIDTH : (i + 1) * WIDTH]) for i in range(3)]
    return token_out, numer_back, denom_back, grads


def back_kernel(
    sharp, assign, ask, look, content, pool, cross, rows_in, x_hbm, probs_hbm,
    score_hbm, numer_out, grads_out,
    x, probs_all, score_all, assign_wide, scale, ones, token_wide, denom_back, small, sum_slice, sum_heat,
    sems, out_sems,
):
    step = pl.program_id(0)
    last = pl.num_programs(0) - 1
    tiles = x.shape[0] // TILE

    def fetches(i):
        t = slice(i * TILE, (i + 1) * TILE)
        return [
            pltpu.make_async_copy(probs_hbm.at[t], probs_all.at[t], sems.at[2 * i]),
            pltpu.make_async_copy(x_hbm.at[t], x.at[t], sems.at[2 * i + 1]),
        ]

    @pl.when(step == 0)
    def _():
        for i in range(tiles):
            for copy in fetches(i):
                copy.start()
        assign_wide[...] = block_slices(assign[...]).astype(BF16)
        scale[...] = sharpness_row(sharp[...])
        ones[...] = head_sums()
        token_out, numer_back, shift, grads = attend_terms(pool, ask, look, content, ones[...])
        token_wide[:, :WIDTH] = stack_heads(token_out).astype(BF16)
        token_wide[:, WIDTH:] = stack_heads(numer_back).astype(BF16)
        denom_back[...] = shift
        small[...] = jnp.zeros_like(small)
        lane = lax.broadcasted_iota(jnp.int32, (D, WIDTH), 1)
        for i, term in enumerate(grads):
            small[:D, :] += jnp.where((lane >> 4) == i, term, 0.0) * (1.0 / 64.0)
        sum_slice[...] = jnp.zeros_like(sum_slice)
        sum_heat[...] = jnp.zeros_like(sum_heat)

    def sends(i):
        t = slice(i * TILE, (i + 1) * TILE)
        return pltpu.make_async_copy(score_all.at[t], score_hbm.at[t], out_sems.at[i])

    for i in range(tiles):

        @pl.when(step == i)
        def _(i=i):
            for copy in fetches(i):
                copy.wait()

    here = pl.ds(pl.multiple_of(step * TILE, TILE), TILE)
    mid = rows_in[:, :WIDTH]
    probs = probs_all[here]
    logits = dot(mid, assign_wide[...]) * scale[...]
    prob_back = dot(rows_in[:, WIDTH:], token_wide[...], 1, 1) + denom_back[...]
    inner = both_halves(group_sum(probs * prob_back, ones[...]))
    logit_back = probs * (prob_back - inner)
    sum_heat[...] += fold_rows(logit_back * logits, 8)
    score_back = (logit_back * scale[...]).astype(BF16)
    score_all[here] = score_back
    for i in range(tiles):

        @pl.when(step == i)
        def _(i=i):
            sends(i).start()

    sum_slice[...] += dot(jnp.concatenate([x[here], mid], 1), score_back, 0, 0)

    @pl.when(step == last)
    def _():
        mid_grad = dot_left(sum_slice[:WIDTH], assign_wide[...], 1)
        tokens = token_wide[:, :WIDTH]
        numers = token_wide[:, WIDTH:]
        cross_high, cross_low = parts(cross[:LANES])
        feat_grad = dot(cross_high[:, :WIDTH], numers, 0, 0) + dot(
            cross_low[:, :WIDTH], numers, 0, 0
        )
        result_grad = dot(tokens, cross_high[:, WIDTH:], 0, 0) + dot(
            tokens, cross_low[:, WIDTH:], 0, 0
        )
        mass_high, mass_low = parts(cross[LANES:])
        mass_rest = (
            cross[LANES:] - mass_high.astype(F32) - mass_low.astype(F32)
        ).astype(BF16)
        bias_grad = dot(mass_high, numers) + dot(mass_low, numers) + dot(mass_rest, numers)
        kept = jnp.where(match((WIDTH, LANES), head16, lane_head), sum_slice[WIDTH:], 0.0)
        row, col = grid_of((LANES, WIDTH))
        kept = dot_left(fold_rows(kept, D), ((row >> 3) + 64 == col).astype(BF16))
        small[:D, :] += kept
        small[D : D + 1, :] = bias_grad[:1]
        heat = jnp.sum(sum_heat[...], 0, keepdims=True) * scale[...]
        heat = jnp.broadcast_to(heat[:, :WIDTH] + heat[:, WIDTH:], (8, WIDTH))
        for width in (64, 32, 16, 8):
            heat = heat + pltpu.roll(heat, width, 1)
        small[D + 1 : D + 2, :] = -heat[:1]
        numer_out[...] = numers
        grads_out[:WIDTH] = mid_grad
        grads_out[WIDTH : 2 * WIDTH] = feat_grad
        grads_out[2 * WIDTH : 3 * WIDTH] = result_grad
        grads_out[3 * WIDTH :] = small[...]
        for i in range(tiles):
            sends(i).wait()


def sense_kernel(
    hidden, aggregate, assign, numers, score, probs, sense_out, weights, assign_wide,
):
    @pl.when(pl.program_id(0) == 0)
    def _():
        weights[:, :WIDTH] = hidden[...]
        weights[:, WIDTH:] = aggregate[...]
        assign_wide[...] = block_slices(assign[...]).astype(BF16)

    mid_back = dot(score[...], assign_wide[...], 1, 1).astype(BF16)
    feat_back = dot(probs[...].astype(BF16), numers[...]).astype(BF16)
    sense_out[...] = dot(jnp.concatenate([mid_back, feat_back], 1), weights[...], 1, 1)


def split_kernel(
    grads, mid_out, feat_out, bias_out, slice_out, heat_out, ask_out, look_out, content_out,
    result_out,
):
    mid_out[...] = grads[:WIDTH]
    feat_out[...] = grads[WIDTH : 2 * WIDTH]
    result_out[...] = grads[2 * WIDTH : 3 * WIDTH]
    small = grads[3 * WIDTH : 3 * WIDTH + 24]
    ask_out[...] = small[:D, 0:D]
    look_out[...] = small[:D, D : 2 * D]
    content_out[...] = small[:D, 2 * D : 3 * D]
    slice_out[...] = small[:D, 64 : 64 + SLICES]
    bias_out[...] = small[D : D + 1, :]
    heat_out[...] = small[D + 1 : D + 2, :HEADS]


def exchange(block, axes, copies):
    sent = jnp.broadcast_to(block[None], (copies,) + block.shape)
    return lax.all_to_all(sent, axes, 0, 0, tiled=True)


def sum_over_nodes(sent):
    part = jnp.sum(lax.all_to_all(sent, ("zh", "core"), 0, 0, tiled=True), 0)
    part = jnp.sum(exchange(part, ("y", "x"), 16), 0)
    return lax.all_gather(part, "core", axis=0, tiled=False)


def sum_over_all(sent):
    sent = sent.reshape(64, GRAD_ROWS // 64, 128)
    part = jnp.sum(lax.all_to_all(sent, BLOCK, 0, 0, tiled=True), 0)
    part = jnp.sum(exchange(part, COLUMN, 8), 0)
    return exchange(part, BLOCK, 64).reshape(GRAD_ROWS, 128)


def whole(shape):
    return pl.BlockSpec(shape, lambda i: (0,) * len(shape))


def tiled(width):
    return pl.BlockSpec((TILE, width), lambda i: (i, 0))


def hbm(a):
    return pltpu.with_memory_space_constraint(a, pltpu.HBM)


def shape(dims, dtype=F32):
    return jax.ShapeDtypeStruct(dims, dtype)


def pool(x, g, hidden, aggregate, offset, assign, sharp, result):
    nodes = x.shape[0]
    return pl.pallas_call(
        pool_kernel,
        grid=(nodes // TILE,),
        in_specs=[
            whole((1, HEADS)),
            tiled(WIDTH), tiled(WIDTH), whole((WIDTH, WIDTH)), whole((WIDTH, WIDTH)),
            whole((1, WIDTH)), whole((D, SLICES)), whole((WIDTH, WIDTH)),
        ],
        out_specs=[tiled(3 * WIDTH), whole((4, SLICES + 1, 128))],
        out_shape=[
            shape((nodes, 3 * WIDTH), BF16), shape((4, SLICES + 1, 128)),
        ],
        scratch_shapes=[
            pltpu.VMEM((WIDTH, LANES), BF16), pltpu.VMEM((WIDTH, LANES), BF16),
            pltpu.VMEM((1, LANES), F32), pltpu.VMEM((LANES, WIDTH), BF16),
            pltpu.VMEM((LANES, LANES), F32), pltpu.VMEM((8, LANES), F32),
        ],
        compiler_params=pltpu.CompilerParams(vmem_limit_bytes=40 << 20),
        name="pool",
    )(*[hbm(a) for a in (sharp, x, g, hidden, aggregate, offset, assign, result)])


def cross(x, g, assign, sharp, rows):
    nodes = x.shape[0]
    raw = pl.BlockSpec(memory_space=pltpu.HBM)
    return pl.pallas_call(
        cross_kernel,
        grid=(nodes // TILE,),
        in_specs=[whole((1, HEADS)), whole((D, SLICES)), tiled(3 * WIDTH), raw, raw],
        out_specs=[whole((LANES + 8, LANES)), raw],
        out_shape=[shape((LANES + 8, LANES)), pltpu.HBM((nodes, LANES), F32)],
        scratch_shapes=[
            pltpu.VMEM((nodes, LANES), BF16), pltpu.VMEM((nodes, LANES), F32),
            pltpu.VMEM((WIDTH, LANES), BF16), pltpu.VMEM((1, LANES), F32),
            pltpu.VMEM((LANES, WIDTH), BF16), pltpu.VMEM((8, LANES), F32),
            pltpu.SemaphoreType.DMA((3 * (nodes // TILE),)),
        ],
        compiler_params=pltpu.CompilerParams(vmem_limit_bytes=40 << 20),
        name="cross",
    )(hbm(sharp), hbm(assign), rows, hbm(x), hbm(g))


def back(pool_sum, crossed, x, assign, sharp, ask, look, content, probs, rows):
    nodes = x.shape[0]
    return pl.pallas_call(
        back_kernel,
        grid=(nodes // TILE,),
        in_specs=[
            whole((1, HEADS)), whole((D, SLICES)), whole((D, D)), whole((D, D)), whole((D, D)),
            whole((2, SLICES + 1, 128)), whole((LANES + 8, LANES)), tiled(3 * WIDTH),
            pl.BlockSpec(memory_space=pltpu.HBM), pl.BlockSpec(memory_space=pltpu.HBM),
        ],
        out_specs=[
            pl.BlockSpec(memory_space=pltpu.HBM), whole((LANES, WIDTH)), whole((GRAD_ROWS, 128)),
        ],
        out_shape=[
            pltpu.HBM((nodes, LANES), BF16), shape((LANES, WIDTH), BF16), shape((GRAD_ROWS, 128)),
        ],
        scratch_shapes=[
            pltpu.VMEM((nodes, WIDTH), BF16), pltpu.VMEM((nodes, LANES), F32),
            pltpu.VMEM((nodes, LANES), BF16),
            pltpu.VMEM((WIDTH, LANES), BF16), pltpu.VMEM((1, LANES), F32),
            pltpu.VMEM((LANES, WIDTH), BF16), pltpu.VMEM((LANES, LANES), BF16),
            pltpu.VMEM((1, LANES), F32), pltpu.VMEM((WIDTH, WIDTH), F32),
            pltpu.VMEM((LANES, LANES), F32), pltpu.VMEM((8, LANES), F32),
            pltpu.SemaphoreType.DMA((2 * (nodes // TILE),)),
            pltpu.SemaphoreType.DMA((nodes // TILE,)),
        ],
        compiler_params=pltpu.CompilerParams(vmem_limit_bytes=40 << 20),
        name="back",
    )(sharp, assign, ask, look, content, pool_sum, crossed, rows, hbm(x), hbm(probs))


def sense(hidden, aggregate, assign, numers, score, probs):
    nodes = score.shape[0]
    square = whole((WIDTH, WIDTH))
    return pl.pallas_call(
        sense_kernel,
        grid=(nodes // TILE,),
        in_specs=[
            square, square, whole((D, SLICES)), whole((LANES, WIDTH)), tiled(LANES), tiled(LANES),
        ],
        out_specs=tiled(WIDTH),
        out_shape=pltpu.HBM((nodes, WIDTH), F32),
        scratch_shapes=[pltpu.VMEM((WIDTH, LANES), BF16), pltpu.VMEM((WIDTH, LANES), BF16)],
        compiler_params=pltpu.CompilerParams(vmem_limit_bytes=40 << 20),
        name="sense",
    )(*[hbm(a) for a in (hidden, aggregate, assign)], numers, hbm(score), hbm(probs))


def split(grads):
    square = (WIDTH, WIDTH)
    outs = [
        square, square, (1, WIDTH), (D, SLICES), (1, HEADS), (D, D), (D, D), (D, D), square,
    ]
    return pl.pallas_call(
        split_kernel,
        out_shape=[shape(s) for s in outs],
        name="split",
    )(pltpu.with_memory_space_constraint(grads, pltpu.VMEM))


def shards(
    vertex_embedding_array,
    result_sensitivity,
    hidden_projection,
    aggregate_projection,
    aggregate_offset,
    assignment_projection,
    softmax_sharpness,
    state_asking_map,
    state_lookup_map,
    state_content_map,
    result_projection,
):
    x = vertex_embedding_array[0]
    g = result_sensitivity[0]
    rows, pooled = pool(
        x, g, hidden_projection, aggregate_projection, aggregate_offset[None],
        assignment_projection, softmax_sharpness[None], result_projection,
    )
    sharp = softmax_sharpness[None]
    pool_sum = sum_over_nodes(pooled)
    crossed, probs = cross(x, g, assignment_projection, sharp, rows)
    score, numers, grads = back(
        pool_sum, crossed, x, assignment_projection, sharp, state_asking_map, state_lookup_map,
        state_content_map, probs, rows,
    )
    nodes_out = sense(
        hidden_projection, aggregate_projection, assignment_projection, numers, score, probs
    )
    mid, feat, bias, slices, heat, ask, look, content, result = split(sum_over_all(grads))
    return nodes_out[None], mid, feat, bias[0], slices, heat[0], ask, look, content, result


def solution(mesh):
    fine = Mesh(mesh.devices.reshape(2, 2, 2, 4, 2, 4, 2), MEMBER + NODE)
    nodes = P(MEMBER, NODE, None)
    return jax.shard_map(
        shards,
        mesh=fine,
        in_specs=(nodes, nodes) + (P(),) * 9,
        out_specs=(nodes,) + (P(),) * 9,
        check_vma=False,
    )
```

```python
import jax
import jax.numpy as jnp
from jax import lax
from jax.experimental import pallas as pl
from jax.experimental.pallas import tpu as pltpu
from jax.sharding import Mesh, PartitionSpec as P

HEADS = 8
SLICES = 32
D = 16
WIDTH = HEADS * D
LANES = HEADS * SLICES
EPS = 1e-05
TILE = 2048
GRAD_ROWS = 512
MEMBER = ("z4", "z2", "z1")
NODE = ("y", "zh", "x", "core")
BLOCK = ("y", "x", "core")
COLUMN = ("z4", "z2", "z1", "zh")
F32 = jnp.float32
BF16 = jnp.bfloat16


def dot(a, b, ca=1, cb=0):
    return lax.dot_general(
        a, b, (((ca,), (cb,)), ((), ())), preferred_element_type=F32
    )


def grid_of(shape):
    return lax.broadcasted_iota(jnp.int32, shape, 0), lax.broadcasted_iota(jnp.int32, shape, 1)


def match(shape, f, g):
    r, c = grid_of(shape)
    return f(r) == g(c)


def head16(i):
    return i >> 4


def in16(i):
    return i & 15


def lane_head(i):
    return i & 7


def lane_slice(i):
    return i >> 3


def same(i):
    return i


def block_slices(a16x32):
    rows = dot(match((WIDTH, D), in16, same).astype(BF16), a16x32).astype(BF16)
    wide = dot(rows, match((SLICES, LANES), same, lane_slice).astype(BF16))
    return jnp.where(match((WIDTH, LANES), head16, lane_head), wide, 0.0)


def block_square(a16x16):
    rows = dot(match((WIDTH, D), in16, same).astype(BF16), a16x16).astype(BF16)
    wide = dot(rows, match((D, WIDTH), same, in16).astype(BF16))
    return jnp.where(match((WIDTH, WIDTH), head16, head16), wide, 0.0)


def sharpness_row(sharp):
    col = lax.broadcasted_iota(jnp.int32, (1, LANES), 1) & 7
    row = jnp.zeros((1, LANES), F32)
    for h in range(HEADS):
        row = jnp.where(col == h, sharp[:, h : h + 1], row)
    return 1.0 / row


def parts(a):
    high = a.astype(BF16)
    return high, (a - high.astype(F32)).astype(BF16)


def head_sums():
    row, col = grid_of((2 * WIDTH, WIDTH))
    return ((row & 7) == (col & 7)).astype(BF16)


def group_sum(a, ones):
    high, low = parts(a[:, :WIDTH] + a[:, WIDTH:])
    return dot(jnp.concatenate([high, low], 1), ones)


def both_halves(a):
    return jnp.concatenate([a, a], 1)


def dot_left(a, b, cb=0):
    high, low = parts(a)
    return dot(jnp.concatenate([high, low], 1), jnp.concatenate([b, b], cb), 1, cb)


def dot_both(a, b, ca=1, cb=0):
    a_high, a_low = parts(a)
    b_high, b_low = parts(b)
    left = jnp.concatenate([a_high, a_high, a_low], ca)
    right = jnp.concatenate([b_high, b_low, b_high], cb)
    return dot(left, right, ca, cb)


def fold_lanes(a):
    for width in (64, 32, 16):
        a = a + pltpu.roll(a, width, 1)
    return a


def fold_rows(a, rows):
    return jnp.sum(a.reshape(a.shape[0] // rows, rows, a.shape[1]), 0)


def stack_heads(a):
    tall = jnp.broadcast_to(a[:, None, :], (SLICES, HEADS, WIDTH)).reshape(LANES, WIDTH)
    return jnp.where(match((LANES, WIDTH), lane_head, head16), tall, 0.0)


def unstack_heads(a):
    return jnp.sum(a.reshape(SLICES, HEADS, a.shape[1]), 1)


def pool_kernel(
    sharp, x, g, hidden, aggregate, offset, assign, result, rows_out, pool_out,
    weights, assign_wide, scale, ones, pooled, mass,
):
    step = pl.program_id(0)

    @pl.when(step == 0)
    def _():
        weights[:, :WIDTH] = hidden[...]
        weights[:, WIDTH:] = aggregate[...]
        assign_wide[...] = block_slices(assign[...]).astype(BF16)
        scale[...] = sharpness_row(sharp[...])
        ones[...] = head_sums()
        pooled[...] = jnp.zeros_like(pooled)
        mass[...] = jnp.zeros_like(mass)

    both = dot(x[...], weights[...])
    mid = both[:, :WIDTH].astype(BF16)
    feat = (both[:, WIDTH:] + offset[...]).astype(BF16)
    back = dot(g[...], result[...], 1, 1).astype(BF16)
    rows_out[:, :WIDTH] = mid
    rows_out[:, WIDTH : 2 * WIDTH] = back
    rows_out[:, 2 * WIDTH :] = feat
    expon = jnp.exp(dot(mid, assign_wide[...]) * scale[...])
    probs = expon * both_halves(1.0 / group_sum(expon, ones[...]))
    mass[...] += fold_rows(probs, 8)
    pooled[...] += dot(probs.astype(BF16), jnp.concatenate([back, feat], 1), 0, 0)

    @pl.when(step == pl.num_programs(0) - 1)
    def _():
        row, col = grid_of((LANES, LANES))
        small = unstack_heads(jnp.where((row & 7) == ((col & 127) >> 4), pooled[...], 0.0))
        total = jnp.sum(mass[...], 0, keepdims=True)
        for z in range(2):
            pool_out[2 * z, :SLICES] = small[:, WIDTH:]
            pool_out[2 * z, SLICES:] = total[:, :WIDTH]
            pool_out[2 * z + 1, :SLICES] = small[:, :WIDTH]
            pool_out[2 * z + 1, SLICES:] = total[:, WIDTH:]


def cross_kernel(
    sharp, assign, rows_in, x_hbm, g_hbm, cross_out, probs_hbm,
    pairs, probs_all, assign_wide, scale, ones, mass, sems,
):
    step = pl.program_id(0)
    tiles = probs_hbm.shape[0] // TILE

    def moves(i):
        t = slice(i * TILE, (i + 1) * TILE)
        return (
            pltpu.make_async_copy(x_hbm.at[t], pairs.at[t, :WIDTH], sems.at[3 * i]),
            pltpu.make_async_copy(g_hbm.at[t], pairs.at[t, WIDTH:], sems.at[3 * i + 1]),
            pltpu.make_async_copy(probs_all.at[t], probs_hbm.at[t], sems.at[3 * i + 2]),
        )

    @pl.when(step == 0)
    def _():
        for i in range(tiles):
            for copy in moves(i)[:2]:
                copy.start()
        assign_wide[...] = block_slices(assign[...]).astype(BF16)
        scale[...] = sharpness_row(sharp[...])
        ones[...] = head_sums()
        cross_out[...] = jnp.zeros_like(cross_out)
        mass[...] = jnp.zeros_like(mass)

    here = pl.ds(pl.multiple_of(step * TILE, TILE), TILE)
    expon = jnp.exp(dot(rows_in[:, :WIDTH], assign_wide[...]) * scale[...])
    probs = expon * both_halves(1.0 / group_sum(expon, ones[...]))
    probs_all[here] = probs
    for i in range(tiles):

        @pl.when(step == i)
        def _(i=i):
            moves(i)[2].start()
            for copy in moves(i)[:2]:
                copy.wait()

    half = probs.astype(BF16)
    mass[...] += fold_rows(half.astype(F32), 8)
    cross_out[:LANES] += dot(half, pairs[here], 0, 0)

    @pl.when(step == tiles - 1)
    def _():
        total = jnp.sum(mass[...], 0, keepdims=True)
        cross_out[LANES:] = jnp.broadcast_to(total, (8, LANES))
        for i in range(tiles):
            moves(i)[2].wait()


def attend_terms(pool, ask, look, content, ones):
    numer = pool[0, :SLICES]
    token_grad = pool[1, :SLICES]
    mass = jnp.concatenate([pool[0, SLICES:], pool[1, SLICES:]], 1)
    spread = jnp.where(match((SLICES, LANES), same, lane_slice), mass, 0.0)
    heads = match((LANES, WIDTH), lane_head, head16)
    heads_half = heads.astype(BF16)
    high, low = parts(spread)
    rest = (spread - high.astype(F32) - low.astype(F32)).astype(BF16)
    denom = dot(jnp.concatenate([high, low, rest], 1), jnp.concatenate([heads_half] * 3, 0)) + EPS
    inverse = 1.0 / denom
    tokens = numer * inverse
    maps = jnp.concatenate([block_square(m[...]) for m in (ask, look, content)], 1).astype(BF16)
    q_k_v = dot_left(tokens, maps)
    q = q_k_v[:, :WIDTH]
    keys = stack_heads(q_k_v[:, WIDTH : 2 * WIDTH])
    values = stack_heads(q_k_v[:, 2 * WIDTH :])
    expon = jnp.exp(dot_both(q, keys, 1, 1) * 0.25)
    rows_back = dot_both(token_grad, values, 1, 1)
    rows = expon * both_halves(1.0 / group_sum(expon, ones))
    token_out = dot_both(rows, values)
    centre = both_halves(group_sum(rows_back * rows, ones))
    scores_back = rows * (rows_back - centre) * 0.25
    q_back = dot_both(scores_back, keys)
    k_back = unstack_heads(jnp.where(heads, dot_both(scores_back, q, 0, 0), 0.0))
    v_back = unstack_heads(jnp.where(heads, dot_both(rows, token_grad, 0, 0), 0.0))
    three = jnp.concatenate([q_back, k_back, v_back], 1)
    tok_back = dot_left(three, maps, 1)
    numer_back = tok_back * inverse
    folded = dot_left(numer_back * tokens, heads_half, 1)
    folded = jnp.where(match((SLICES, LANES), same, lane_slice), folded, 0.0)
    denom_back = -jnp.sum(folded, 0, keepdims=True)
    row, col = grid_of((WIDTH, 3 * WIDTH))
    wide = jnp.where((row >> 4) == ((col & 127) >> 4), dot_both(tokens, three, 0, 0), 0.0)
    wide = fold_rows(wide, D)
    grads = [fold_lanes(wide[:, i * WIDTH : (i + 1) * WIDTH]) for i in range(3)]
    return token_out, numer_back, denom_back, grads


def back_kernel(
    sharp, assign, ask, look, content, pool, cross, rows_in, x_hbm, probs_hbm,
    score_hbm, numer_out, grads_out,
    x, probs_all, score_all, assign_wide, scale, ones, token_wide, denom_back, small, sum_slice, sum_heat,
    sems, out_sems,
):
    step = pl.program_id(0)
    last = pl.num_programs(0) - 1
    tiles = x.shape[0] // TILE

    def fetches(i):
        t = slice(i * TILE, (i + 1) * TILE)
        return [
            pltpu.make_async_copy(probs_hbm.at[t], probs_all.at[t], sems.at[2 * i]),
            pltpu.make_async_copy(x_hbm.at[t], x.at[t], sems.at[2 * i + 1]),
        ]

    @pl.when(step == 0)
    def _():
        for i in range(tiles):
            for copy in fetches(i):
                copy.start()
        assign_wide[...] = block_slices(assign[...]).astype(BF16)
        scale[...] = sharpness_row(sharp[...])
        ones[...] = head_sums()
        token_out, numer_back, shift, grads = attend_terms(pool, ask, look, content, ones[...])
        token_wide[:, :WIDTH] = stack_heads(token_out).astype(BF16)
        token_wide[:, WIDTH:] = stack_heads(numer_back).astype(BF16)
        denom_back[...] = shift
        small[...] = jnp.zeros_like(small)
        lane = lax.broadcasted_iota(jnp.int32, (D, WIDTH), 1)
        for i, term in enumerate(grads):
            small[:D, :] += jnp.where((lane >> 4) == i, term, 0.0) * (1.0 / 64.0)
        sum_slice[...] = jnp.zeros_like(sum_slice)
        sum_heat[...] = jnp.zeros_like(sum_heat)

    def sends(i):
        t = slice(i * TILE, (i + 1) * TILE)
        return pltpu.make_async_copy(score_all.at[t], score_hbm.at[t], out_sems.at[i])

    for i in range(tiles):

        @pl.when(step == i)
        def _(i=i):
            for copy in fetches(i):
                copy.wait()

    here = pl.ds(pl.multiple_of(step * TILE, TILE), TILE)
    mid = rows_in[:, :WIDTH]
    probs = probs_all[here]
    logits = dot(mid, assign_wide[...]) * scale[...]
    prob_back = dot(rows_in[:, WIDTH:], token_wide[...], 1, 1) + denom_back[...]
    inner = both_halves(group_sum(probs * prob_back, ones[...]))
    logit_back = probs * (prob_back - inner)
    sum_heat[...] += fold_rows(logit_back * logits, 8)
    score_back = (logit_back * scale[...]).astype(BF16)
    score_all[here] = score_back
    for i in range(tiles):

        @pl.when(step == i)
        def _(i=i):
            sends(i).start()

    sum_slice[...] += dot(jnp.concatenate([x[here], mid], 1), score_back, 0, 0)

    @pl.when(step == last)
    def _():
        mid_grad = dot_left(sum_slice[:WIDTH], assign_wide[...], 1)
        tokens = token_wide[:, :WIDTH]
        numers = token_wide[:, WIDTH:]
        cross_high, cross_low = parts(cross[:LANES])
        feat_grad = dot(cross_high[:, :WIDTH], numers, 0, 0) + dot(
            cross_low[:, :WIDTH], numers, 0, 0
        )
        result_grad = dot(tokens, cross_high[:, WIDTH:], 0, 0) + dot(
            tokens, cross_low[:, WIDTH:], 0, 0
        )
        mass_high, mass_low = parts(cross[LANES:])
        mass_rest = (
            cross[LANES:] - mass_high.astype(F32) - mass_low.astype(F32)
        ).astype(BF16)
        bias_grad = dot(mass_high, numers) + dot(mass_low, numers) + dot(mass_rest, numers)
        kept = jnp.where(match((WIDTH, LANES), head16, lane_head), sum_slice[WIDTH:], 0.0)
        row, col = grid_of((LANES, WIDTH))
        kept = dot_left(fold_rows(kept, D), ((row >> 3) + 64 == col).astype(BF16))
        small[:D, :] += kept
        small[D : D + 1, :] = bias_grad[:1]
        heat = jnp.sum(sum_heat[...], 0, keepdims=True) * scale[...]
        heat = jnp.broadcast_to(heat[:, :WIDTH] + heat[:, WIDTH:], (8, WIDTH))
        for width in (64, 32, 16, 8):
            heat = heat + pltpu.roll(heat, width, 1)
        small[D + 1 : D + 2, :] = -heat[:1]
        numer_out[...] = numers
        grads_out[:WIDTH] = mid_grad
        grads_out[WIDTH : 2 * WIDTH] = feat_grad
        grads_out[2 * WIDTH : 3 * WIDTH] = result_grad
        grads_out[3 * WIDTH :] = small[...]
        for i in range(tiles):
            sends(i).wait()


def sense_kernel(
    hidden, aggregate, assign, numers, score, probs, sense_out, weights, assign_wide,
):
    @pl.when(pl.program_id(0) == 0)
    def _():
        weights[:, :WIDTH] = hidden[...]
        weights[:, WIDTH:] = aggregate[...]
        assign_wide[...] = block_slices(assign[...]).astype(BF16)

    mid_back = dot(score[...], assign_wide[...], 1, 1).astype(BF16)
    feat_back = dot(probs[...].astype(BF16), numers[...]).astype(BF16)
    sense_out[...] = dot(jnp.concatenate([mid_back, feat_back], 1), weights[...], 1, 1)


def split_kernel(
    grads, mid_out, feat_out, bias_out, slice_out, heat_out, ask_out, look_out, content_out,
    result_out,
):
    mid_out[...] = grads[:WIDTH]
    feat_out[...] = grads[WIDTH : 2 * WIDTH]
    result_out[...] = grads[2 * WIDTH : 3 * WIDTH]
    small = grads[3 * WIDTH : 3 * WIDTH + 24]
    ask_out[...] = small[:D, 0:D]
    look_out[...] = small[:D, D : 2 * D]
    content_out[...] = small[:D, 2 * D : 3 * D]
    slice_out[...] = small[:D, 64 : 64 + SLICES]
    bias_out[...] = small[D : D + 1, :]
    heat_out[...] = small[D + 1 : D + 2, :HEADS]


def exchange(block, axes, copies):
    sent = jnp.broadcast_to(block[None], (copies,) + block.shape)
    return lax.all_to_all(sent, axes, 0, 0, tiled=True)


def sum_over_nodes(sent):
    part = jnp.sum(lax.all_to_all(sent, ("zh", "core"), 0, 0, tiled=True), 0)
    part = jnp.sum(exchange(part, ("y", "x"), 16), 0)
    return lax.all_gather(part, "core", axis=0, tiled=False)


def sum_over_all(sent):
    sent = sent.reshape(32, GRAD_ROWS // 32, 128)
    part = jnp.sum(lax.all_to_all(sent, BLOCK, 0, 0, tiled=True), 0)
    part = jnp.sum(exchange(part, COLUMN, 16), 0)
    return exchange(part, BLOCK, 32).reshape(GRAD_ROWS, 128)


def whole(shape):
    return pl.BlockSpec(shape, lambda i: (0,) * len(shape))


def tiled(width):
    return pl.BlockSpec((TILE, width), lambda i: (i, 0))


def hbm(a):
    return pltpu.with_memory_space_constraint(a, pltpu.HBM)


def shape(dims, dtype=F32):
    return jax.ShapeDtypeStruct(dims, dtype)


def pool(x, g, hidden, aggregate, offset, assign, sharp, result):
    nodes = x.shape[0]
    return pl.pallas_call(
        pool_kernel,
        grid=(nodes // TILE,),
        in_specs=[
            whole((1, HEADS)),
            tiled(WIDTH), tiled(WIDTH), whole((WIDTH, WIDTH)), whole((WIDTH, WIDTH)),
            whole((1, WIDTH)), whole((D, SLICES)), whole((WIDTH, WIDTH)),
        ],
        out_specs=[tiled(3 * WIDTH), whole((4, SLICES + 1, 128))],
        out_shape=[
            shape((nodes, 3 * WIDTH), BF16), shape((4, SLICES + 1, 128)),
        ],
        scratch_shapes=[
            pltpu.VMEM((WIDTH, LANES), BF16), pltpu.VMEM((WIDTH, LANES), BF16),
            pltpu.VMEM((1, LANES), F32), pltpu.VMEM((LANES, WIDTH), BF16),
            pltpu.VMEM((LANES, LANES), F32), pltpu.VMEM((8, LANES), F32),
        ],
        compiler_params=pltpu.CompilerParams(vmem_limit_bytes=40 << 20),
        name="pool",
    )(*[hbm(a) for a in (sharp, x, g, hidden, aggregate, offset, assign, result)])


def cross(x, g, assign, sharp, rows):
    nodes = x.shape[0]
    raw = pl.BlockSpec(memory_space=pltpu.HBM)
    return pl.pallas_call(
        cross_kernel,
        grid=(nodes // TILE,),
        in_specs=[whole((1, HEADS)), whole((D, SLICES)), tiled(3 * WIDTH), raw, raw],
        out_specs=[whole((LANES + 8, LANES)), raw],
        out_shape=[shape((LANES + 8, LANES)), pltpu.HBM((nodes, LANES), F32)],
        scratch_shapes=[
            pltpu.VMEM((nodes, LANES), BF16), pltpu.VMEM((nodes, LANES), F32),
            pltpu.VMEM((WIDTH, LANES), BF16), pltpu.VMEM((1, LANES), F32),
            pltpu.VMEM((LANES, WIDTH), BF16), pltpu.VMEM((8, LANES), F32),
            pltpu.SemaphoreType.DMA((3 * (nodes // TILE),)),
        ],
        compiler_params=pltpu.CompilerParams(vmem_limit_bytes=40 << 20),
        name="cross",
    )(hbm(sharp), hbm(assign), rows, hbm(x), hbm(g))


def back(pool_sum, crossed, x, assign, sharp, ask, look, content, probs, rows):
    nodes = x.shape[0]
    return pl.pallas_call(
        back_kernel,
        grid=(nodes // TILE,),
        in_specs=[
            whole((1, HEADS)), whole((D, SLICES)), whole((D, D)), whole((D, D)), whole((D, D)),
            whole((2, SLICES + 1, 128)), whole((LANES + 8, LANES)), tiled(3 * WIDTH),
            pl.BlockSpec(memory_space=pltpu.HBM), pl.BlockSpec(memory_space=pltpu.HBM),
        ],
        out_specs=[
            pl.BlockSpec(memory_space=pltpu.HBM), whole((LANES, WIDTH)), whole((GRAD_ROWS, 128)),
        ],
        out_shape=[
            pltpu.HBM((nodes, LANES), BF16), shape((LANES, WIDTH), BF16), shape((GRAD_ROWS, 128)),
        ],
        scratch_shapes=[
            pltpu.VMEM((nodes, WIDTH), BF16), pltpu.VMEM((nodes, LANES), F32),
            pltpu.VMEM((nodes, LANES), BF16),
            pltpu.VMEM((WIDTH, LANES), BF16), pltpu.VMEM((1, LANES), F32),
            pltpu.VMEM((LANES, WIDTH), BF16), pltpu.VMEM((LANES, LANES), BF16),
            pltpu.VMEM((1, LANES), F32), pltpu.VMEM((WIDTH, WIDTH), F32),
            pltpu.VMEM((LANES, LANES), F32), pltpu.VMEM((8, LANES), F32),
            pltpu.SemaphoreType.DMA((2 * (nodes // TILE),)),
            pltpu.SemaphoreType.DMA((nodes // TILE,)),
        ],
        compiler_params=pltpu.CompilerParams(vmem_limit_bytes=40 << 20),
        name="back",
    )(sharp, assign, ask, look, content, pool_sum, crossed, rows, hbm(x), hbm(probs))


def sense(hidden, aggregate, assign, numers, score, probs):
    nodes = score.shape[0]
    square = whole((WIDTH, WIDTH))
    return pl.pallas_call(
        sense_kernel,
        grid=(nodes // TILE,),
        in_specs=[
            square, square, whole((D, SLICES)), whole((LANES, WIDTH)), tiled(LANES), tiled(LANES),
        ],
        out_specs=tiled(WIDTH),
        out_shape=pltpu.HBM((nodes, WIDTH), F32),
        scratch_shapes=[pltpu.VMEM((WIDTH, LANES), BF16), pltpu.VMEM((WIDTH, LANES), BF16)],
        compiler_params=pltpu.CompilerParams(vmem_limit_bytes=40 << 20),
        name="sense",
    )(*[hbm(a) for a in (hidden, aggregate, assign)], numers, hbm(score), hbm(probs))


def split(grads):
    square = (WIDTH, WIDTH)
    outs = [
        square, square, (1, WIDTH), (D, SLICES), (1, HEADS), (D, D), (D, D), (D, D), square,
    ]
    return pl.pallas_call(
        split_kernel,
        out_shape=[shape(s) for s in outs],
        name="split",
    )(pltpu.with_memory_space_constraint(grads, pltpu.VMEM))


def shards(
    vertex_embedding_array,
    result_sensitivity,
    hidden_projection,
    aggregate_projection,
    aggregate_offset,
    assignment_projection,
    softmax_sharpness,
    state_asking_map,
    state_lookup_map,
    state_content_map,
    result_projection,
):
    x = vertex_embedding_array[0]
    g = result_sensitivity[0]
    rows, pooled = pool(
        x, g, hidden_projection, aggregate_projection, aggregate_offset[None],
        assignment_projection, softmax_sharpness[None], result_projection,
    )
    sharp = softmax_sharpness[None]
    pool_sum = sum_over_nodes(pooled)
    crossed, probs = cross(x, g, assignment_projection, sharp, rows)
    score, numers, grads = back(
        pool_sum, crossed, x, assignment_projection, sharp, state_asking_map, state_lookup_map,
        state_content_map, probs, rows,
    )
    nodes_out = sense(
        hidden_projection, aggregate_projection, assignment_projection, numers, score, probs
    )
    mid, feat, bias, slices, heat, ask, look, content, result = split(sum_over_all(grads))
    return nodes_out[None], mid, feat, bias[0], slices, heat[0], ask, look, content, result


def solution(mesh):
    fine = Mesh(mesh.devices.reshape(2, 2, 2, 4, 2, 4, 2), MEMBER + NODE)
    nodes = P(MEMBER, NODE, None)
    return jax.shard_map(
        shards,
        mesh=fine,
        in_specs=(nodes, nodes) + (P(),) * 9,
        out_specs=(nodes,) + (P(),) * 9,
        check_vma=False,
    )
```
